32 devices in a mesh: dp: 2 (over x), row: 4 (over z), col: 4 (over y, core).
Axes of the slice: x: 2, y: 2, z: 4, core: 2. Of those that a mesh axis runs over, the one named last changes fastest.
Arguments:
- inputs: bfloat16 [1458, 1152], P('dp', 'row'), may hold values from -40 to 40
- pre_gain: float32 [1152], P('row'), may hold values from 0.5 to 1.5
- pre_shift: float32 [1152], P('row'), may hold values from -1.5 to 1.5
- joint_weight: bfloat16 [1152, 3456], P('row', 'col'), may hold values from -0.1875 to 0.1875
- joint_bias: float32 [4, 4, 144], P('col', 'row'), may hold values from -0.5 to 0.5
- merge_weight: bfloat16 [1152, 1152], P('col', 'row'), may hold values from -4 to 4
- merge_bias: float32 [1152], P('row'), may hold values from -2.5 to 2.5
- mid_gain: float32 [1152], P('row'), may hold values from 0.5 to 1.5
- mid_shift: float32 [1152], P('row'), may hold values from -1.5 to 1.5
- expand_weight: bfloat16 [1152, 4304], P('row', 'col'), may hold values from -0.1875 to 0.1875
- expand_bias: float32 [4304], P('col'), may hold values from -1.5 to 1.5
- reduce_weight: bfloat16 [4304, 1152], P('col', 'row'), may hold values from -0.09375 to 0.09375
- reduce_bias: float32 [1152], P('row'), may hold values from -2.5 to 2.5
- cotangent: bfloat16 [1458, 1152], P('dp', 'row'), may hold values from -6 to 6
Outputs:
- outputs: bfloat16 [1458, 1152], P('dp', 'row')
- inputs_grad: float32 [1458, 1152], P('dp', 'row')
- pre_gain_grad: float32 [1152], P('row')
- pre_shift_grad: float32 [1152], P('row')
- joint_weight_grad: float32 [1152, 3456], P('row', 'col')
- joint_bias_grad: float32 [4, 4, 144], P('col', 'row')
- merge_weight_grad: float32 [1152, 1152], P('col', 'row')
- merge_bias_grad: float32 [1152], P('row')
- mid_gain_grad: float32 [1152], P('row')
- mid_shift_grad: float32 [1152], P('row')
- expand_weight_grad: float32 [1152, 4304], P('row', 'col')
- expand_bias_grad: float32 [4304], P('col')
- reduce_weight_grad: float32 [4304, 1152], P('col', 'row')
- reduce_bias_grad: float32 [1152], P('row')
The draws below stay inside these ranges and needn't reach their ends.
All inputs are finite; a program needn't handle non-finite values.
Results may differ from the reference program's by a relative error of at most 0.015.
Values may be sent and summed in bfloat16 or wider, within the bound.
No kernel may reach another device: no remote copies, remote signals or barrier semaphores. Data moves between devices by JAX's collectives and lax.ppermute only.
A program may use at most 64 MiB of HBM per device.

```python
import math
import jax
import jax.numpy as jnp
from jax import lax

D = 1152
H = 16
HD = 72
FF = 4304
SEQ = 729
IMAGES = 2
TOKENS = 1458
GROUP_HEADS = 4
N_COL = 4


def draw_inputs(key, part):
    first_key, second_key = jax.random.split(key, 2)
    column_scale = jnp.exp(jax.random.uniform(second_key, (1, D), jnp.float32, 0.0, 1.0) * math.log(10.0)) / math.sqrt(10.0)
    values = jax.random.normal(first_key, (TOKENS, D), jnp.float32) * column_scale
    return jnp.clip(values, -40.0, 40.0).astype(jnp.bfloat16)


def block_levels(own_key, extent, cuts, least, top_value):
    loudness = 1.0
    for position, shards_of in cuts:
        steps = jax.random.uniform(jax.random.fold_in(jax.random.fold_in(own_key, 6), position), (shards_of,), jnp.float32, least / len(cuts), top_value / len(cuts))
        loudness = loudness * jnp.repeat(jnp.exp(steps), extent[position] // shards_of).reshape((-1,) + (1,) * (len(extent) - 1 - position))
    return loudness


def bell_draw(key, dims, scale, reach, pieces=(), dtype=jnp.bfloat16):
    entries = jax.random.normal(key, dims, jnp.float32) * scale
    if len(pieces) > 0:
        entries = block_levels(key, dims, pieces, -0.22, 0.18) * entries
    return jnp.clip(entries, min=-reach, max=reach).astype(dtype)


def setup_inputs(seed: int = 0) -> dict:
    seeds = jax.random.split(jax.random.key(seed), 15)
    return {
        "inputs": draw_inputs(jax.random.fold_in(seeds[14], 71), 0),
        "pre_gain": jnp.clip(1.0 + 0.1 * jax.random.normal(seeds[1], (D,), jnp.float32), 0.5, 1.5),
        "pre_shift": bell_draw(seeds[2], (D,), 0.3, 1.5, ((0, 4),), jnp.float32),
        "joint_weight": bell_draw(seeds[3], (D, 3 * D), D ** -0.5, 0.1875, ((0, 4), (1, 4))),
        "joint_bias": bell_draw(seeds[4], (N_COL, GROUP_HEADS, 2 * HD), 0.1, 0.5, ((0, 4), (1, 4)), jnp.float32),
        "merge_weight": bell_draw(seeds[5], (D, D), (D // SEQ + 1) ** -0.5, 4.0, ((0, 4), (1, 4))),
        "merge_bias": bell_draw(seeds[6], (D,), 0.5, 2.5, ((0, 4),), jnp.float32),
        "mid_gain": jnp.clip(1.0 + 0.1 * jax.random.normal(seeds[7], (D,), jnp.float32), 0.5, 1.5),
        "mid_shift": bell_draw(seeds[8], (D,), 0.3, 1.5, ((0, 4),), jnp.float32),
        "expand_weight": bell_draw(seeds[9], (D, FF), D ** -0.5, 0.1875, ((0, 4), (1, 4))),
        "expand_bias": bell_draw(seeds[10], (FF,), 0.3, 1.5, ((0, 4),), jnp.float32),
        "reduce_weight": bell_draw(seeds[11], (FF, D), FF ** -0.5, 0.09375, ((0, 4), (1, 4))),
        "reduce_bias": bell_draw(seeds[12], (D,), 0.5, 2.5, ((0, 4),), jnp.float32),
        "cotangent": bell_draw(seeds[13], (TOKENS, D), 1.0, 6.0, ((0, 2), (1, 4))),
    }


NORM_EPSILON = 1e-06
TANH_SLOPE = 0.7978845608028654
CUBIC_TERM = 0.044715

def round_low(values):
    return lax.optimization_barrier(values.astype(jnp.bfloat16))

def gelu_value(preact):
    return 0.5 * preact * (1.0 + jnp.tanh(TANH_SLOPE * (preact + CUBIC_TERM * preact * preact * preact)))

def gelu_slope(preact):
    inner_tanh = jnp.tanh(TANH_SLOPE * (preact + CUBIC_TERM * preact * preact * preact))
    return 0.5 * (1.0 + inner_tanh) + 0.5 * preact * (1.0 - inner_tanh * inner_tanh) * TANH_SLOPE * (1.0 + 3.0 * CUBIC_TERM * preact * preact)

def norm_forward(values, norm_gain, norm_shift):
    row_mean = lax.optimization_barrier(jnp.mean(values, axis=-1, keepdims=True))
    row_var = lax.optimization_barrier(jnp.mean(values * values, axis=-1, keepdims=True)) - row_mean * row_mean
    inv_scale = lax.rsqrt(row_var + NORM_EPSILON)
    unit_rows = (values - row_mean) * inv_scale
    return (unit_rows, inv_scale, unit_rows * norm_gain + norm_shift)

def norm_backward(upstream, unit_rows, inv_scale, norm_gain):
    scaled = upstream * norm_gain
    first = lax.optimization_barrier(jnp.mean(scaled, axis=-1, keepdims=True))
    second = lax.optimization_barrier(jnp.mean(scaled * unit_rows, axis=-1, keepdims=True))
    return inv_scale * (scaled - first - unit_rows * second)

def attend_image(query_rows, key_rows, value_rows):
    factor = query_rows.shape[-1] ** (-0.5)
    scores = jnp.einsum('qhd,khd->hqk', query_rows.astype(jnp.float32), key_rows.astype(jnp.float32)) * factor
    totals = jnp.log(lax.optimization_barrier(jnp.sum(jnp.exp(scores), axis=-1)))
    softmax_rows = round_low(jnp.exp(scores - totals[..., None]))
    context = jnp.einsum('hqk,khd->qhd', softmax_rows.astype(jnp.float32), value_rows.astype(jnp.float32))
    return (round_low(context), totals)

def attend_back(query_rows, key_rows, value_rows, context, totals, upstream):
    factor = query_rows.shape[-1] ** (-0.5)
    query_wide = query_rows.astype(jnp.float32)
    key_wide = key_rows.astype(jnp.float32)
    value_wide = value_rows.astype(jnp.float32)
    upstream_wide = upstream.astype(jnp.float32)
    scores = jnp.einsum('qhd,khd->hqk', query_wide, key_wide) * factor
    weights = jnp.exp(scores - totals[..., None])
    weights_low = round_low(weights).astype(jnp.float32)
    value_grad = jnp.einsum('hqk,qhd->khd', weights_low, upstream_wide)
    prob_grad = jnp.einsum('qhd,khd->hqk', upstream_wide, value_wide)
    row_delta = jnp.einsum('qhd,qhd->hq', upstream_wide, context.astype(jnp.float32))
    score_grad = round_low(weights * (prob_grad - row_delta[..., None])).astype(jnp.float32)
    query_grad = jnp.einsum('hqk,khd->qhd', score_grad, key_wide) * factor
    key_grad = jnp.einsum('hqk,qhd->khd', score_grad, query_wide) * factor
    return (query_grad, key_grad, value_grad)

def reference(inputs, pre_gain, pre_shift, joint_weight, joint_bias, merge_weight, merge_bias, mid_gain, mid_shift, expand_weight, expand_bias, reduce_weight, reduce_bias, cotangent):
    float_type = jnp.float32
    residual = inputs.astype(float_type)
    unit_first, scale_first, normed_first = norm_forward(residual, pre_gain, pre_shift)
    normed_first = round_low(normed_first)
    bias_pairs = joint_bias.reshape(H, 2 * HD)
    bias_rows = jnp.concatenate([bias_pairs[:, :HD], jnp.zeros((H, HD), float_type), bias_pairs[:, HD:]], axis=1).reshape(3 * D)
    joint_rows = round_low(jnp.dot(normed_first, joint_weight, preferred_element_type=float_type) + bias_rows)
    per_head = joint_rows.reshape(IMAGES, SEQ, H, 3 * HD)
    query_rows = per_head[..., :HD]
    key_rows = per_head[..., HD:2 * HD]
    value_rows = per_head[..., 2 * HD:]
    context, totals = lax.map(lambda packed: attend_image(packed[0], packed[1], packed[2]), (query_rows, key_rows, value_rows))
    context_flat = context.reshape(TOKENS, D)
    mixed_first = residual + jnp.dot(context_flat, merge_weight, preferred_element_type=float_type) + merge_bias
    unit_second, scale_second, normed_second = norm_forward(mixed_first, mid_gain, mid_shift)
    normed_second = round_low(normed_second)
    hidden_pre = jnp.dot(normed_second, expand_weight, preferred_element_type=float_type) + expand_bias
    active = round_low(gelu_value(hidden_pre))
    outputs = (mixed_first + jnp.dot(active, reduce_weight, preferred_element_type=float_type) + reduce_bias).astype(jnp.bfloat16)
    grad_out = cotangent.astype(float_type)
    reduce_weight_grad = jnp.dot(active.T, cotangent, preferred_element_type=float_type)
    reduce_bias_grad = lax.optimization_barrier(jnp.sum(grad_out, axis=0))
    active_grad = jnp.dot(cotangent, reduce_weight.T, preferred_element_type=float_type)
    hidden_grad = round_low(active_grad * gelu_slope(hidden_pre))
    expand_weight_grad = jnp.dot(normed_second.T, hidden_grad, preferred_element_type=float_type)
    expand_bias_grad = lax.optimization_barrier(jnp.sum(hidden_grad.astype(float_type), axis=0))
    normed_second_grad = jnp.dot(hidden_grad, expand_weight.T, preferred_element_type=float_type)
    mid_gain_grad = lax.optimization_barrier(jnp.sum(normed_second_grad * unit_second, axis=0))
    mid_shift_grad = lax.optimization_barrier(jnp.sum(normed_second_grad, axis=0))
    mixed_grad = grad_out + norm_backward(normed_second_grad, unit_second, scale_second, mid_gain)
    mixed_low = round_low(mixed_grad)
    merge_weight_grad = jnp.dot(context_flat.T, mixed_low, preferred_element_type=float_type)
    merge_bias_grad = lax.optimization_barrier(jnp.sum(mixed_grad, axis=0))
    context_grad = round_low(jnp.dot(mixed_low, merge_weight.T, preferred_element_type=float_type))
    context_grad = context_grad.reshape(IMAGES, SEQ, H, HD)
    query_grad, key_grad, value_grad = lax.map(lambda packed: attend_back(packed[0], packed[1], packed[2], packed[3], packed[4], packed[5]), (query_rows, key_rows, value_rows, context, totals, context_grad))
    joint_grad = round_low(jnp.concatenate([query_grad, key_grad, value_grad], axis=-1)).reshape(TOKENS, 3 * D)
    joint_bias_grad = jnp.concatenate([lax.optimization_barrier(jnp.sum(query_grad, axis=(0, 1))), lax.optimization_barrier(jnp.sum(value_grad, axis=(0, 1)))], axis=-1).reshape(N_COL, H // N_COL, 2 * HD)
    joint_weight_grad = jnp.dot(normed_first.T, joint_grad, preferred_element_type=float_type)
    normed_first_grad = jnp.dot(joint_grad, joint_weight.T, preferred_element_type=float_type)
    pre_gain_grad = lax.optimization_barrier(jnp.sum(normed_first_grad * unit_first, axis=0))
    pre_shift_grad = lax.optimization_barrier(jnp.sum(normed_first_grad, axis=0))
    inputs_grad = mixed_grad + norm_backward(normed_first_grad, unit_first, scale_first, pre_gain)
    return (outputs, inputs_grad, pre_gain_grad, pre_shift_grad, joint_weight_grad, joint_bias_grad, merge_weight_grad, merge_bias_grad, mid_gain_grad, mid_shift_grad, expand_weight_grad, expand_bias_grad, reduce_weight_grad, reduce_bias_grad)
```

```python
import jax
import jax.numpy as jnp
from jax import lax
from jax.sharding import PartitionSpec as P

D = 1152
SEQ = 729


NORM_EPSILON = 1e-06
TANH_SLOPE = 0.7978845608028654
CUBIC_TERM = 0.044715
LOW = jnp.bfloat16
WIDE = jnp.float32


def gelu_pair(preact):
    inner_tanh = jnp.tanh(TANH_SLOPE * (preact + CUBIC_TERM * preact * preact * preact))
    value = 0.5 * preact * (1.0 + inner_tanh)
    slope = 0.5 * (1.0 + inner_tanh) + 0.5 * preact * (
        1.0 - inner_tanh * inner_tanh
    ) * TANH_SLOPE * (1.0 + 3.0 * CUBIC_TERM * preact * preact)
    return value, slope


def dot(left, right, left_dim, right_dim):
    return lax.dot_general(
        left, right, (((left_dim,), (right_dim,)), ((), ())), preferred_element_type=WIDE
    )


def pick(blocks, index, axis=0):
    return lax.dynamic_index_in_dim(blocks, index, axis, keepdims=False)


def place(blocks, block, index):
    return lax.dynamic_update_index_in_dim(blocks, block, index, 0)


def after(values, *others):
    return lax.optimization_barrier((values,) + others)[0]


def norm_forward(values):
    row_mean = jnp.mean(values, axis=-1, keepdims=True)
    row_var = jnp.mean(values * values, axis=-1, keepdims=True) - row_mean * row_mean
    inv_scale = lax.rsqrt(row_var + NORM_EPSILON)
    return (values - row_mean) * inv_scale, inv_scale


def norm_backward(upstream, unit_rows, inv_scale, norm_gain):
    scaled = upstream * norm_gain
    first = jnp.mean(scaled, axis=-1, keepdims=True)
    second = jnp.mean(scaled * unit_rows, axis=-1, keepdims=True)
    return inv_scale * (scaled - first - unit_rows * second)


def attend(query_rows, key_rows, value_rows):
    factor = query_rows.shape[-1] ** (-0.5)
    scores = jnp.einsum("iqd,ikd->iqk", query_rows, key_rows, preferred_element_type=WIDE) * factor
    totals = jnp.log(jnp.sum(jnp.exp(scores), axis=-1))
    softmax_rows = jnp.exp(scores - totals[..., None]).astype(LOW)
    context = jnp.einsum("iqk,ikd->iqd", softmax_rows, value_rows, preferred_element_type=WIDE)
    return context.astype(LOW), totals


def attend_back(query_rows, key_rows, value_rows, context, totals, upstream):
    factor = query_rows.shape[-1] ** (-0.5)
    scores = jnp.einsum("iqd,ikd->iqk", query_rows, key_rows, preferred_element_type=WIDE) * factor
    weights = jnp.exp(scores - totals[..., None])
    value_grad = jnp.einsum(
        "iqk,iqd->ikd", weights.astype(LOW), upstream, preferred_element_type=WIDE
    )
    prob_grad = jnp.einsum("iqd,ikd->iqk", upstream, value_rows, preferred_element_type=WIDE)
    row_delta = jnp.sum(upstream.astype(WIDE) * context.astype(WIDE), axis=-1)
    score_grad = (weights * (prob_grad - row_delta[..., None])).astype(LOW)
    query_grad = (
        jnp.einsum("iqk,ikd->iqd", score_grad, key_rows, preferred_element_type=WIDE) * factor
    )
    key_grad = (
        jnp.einsum("iqk,iqd->ikd", score_grad, query_rows, preferred_element_type=WIDE) * factor
    )
    return query_grad, key_grad, value_grad


def make_body(n_dp, n_row, n_col):
    masks = []
    while (1 << len(masks)) < n_col:
        masks.append(1 << len(masks))
    paired = n_dp == 2

    def row_shift(value, step):
        if step == 0:
            return value
        return lax.ppermute(value, "row", [(i, (i + step) % n_row) for i in range(n_row)])

    def col_swap(value, mask):
        return lax.ppermute(value, "col", [(i, i ^ mask) for i in range(n_col)])

    def dp_swap(value):
        return lax.ppermute(value, "dp", [(0, 1), (1, 0)])

    def dp_sum(value):
        if n_dp == 1:
            return value
        return value + dp_swap(value) if paired else lax.psum(value, "dp")

    def row_all(value):
        return [row_shift(value, k) for k in range(n_row)]

    def row_place(pieces, row):
        blocks = jnp.zeros((n_row,) + pieces[0].shape, pieces[0].dtype)
        for k, piece in enumerate(pieces):
            blocks = place(blocks, piece, (row - k) % n_row)
        return blocks

    def col_all(value, col):
        blocks = jnp.zeros((n_col,) + value.shape, value.dtype)
        blocks = place(blocks, value, col)
        held = [(value, 0)]
        for mask in reversed(masks):
            sent = jnp.stack([v for v, _ in held]) if len(held) > 1 else held[0][0][None]
            got = col_swap(sent, mask)
            fresh = []
            for i, (_, offset) in enumerate(held):
                fresh.append((got[i], offset ^ mask))
                blocks = place(blocks, got[i], col ^ (offset ^ mask))
            held = held + fresh
        return blocks

    def roll_blocks(rows, step):
        if step == 0:
            return rows
        width = rows.shape[-1] // n_row
        cut = (n_row - step) * width
        return jnp.concatenate([rows[..., cut:], rows[..., :cut]], axis=-1)

    def body(
        inputs,
        pre_gain,
        pre_shift,
        joint_weight,
        joint_bias,
        merge_weight,
        merge_bias,
        mid_gain,
        mid_shift,
        expand_weight,
        expand_bias,
        reduce_weight,
        reduce_bias,
        cotangent,
    ):
        row = lax.axis_index("row")
        col = lax.axis_index("col")
        rank = lax.axis_index("dp")
        tokens, feats = inputs.shape
        width = feats * n_row
        images = tokens // SEQ
        head_size = joint_bias.shape[2] // 2
        span = -(-tokens // (n_row * n_col * 16)) * 16
        padded = span * n_row * n_col
        block = span * n_row
        units = expand_weight.shape[1] // n_row
        trio = joint_weight.shape[1] // n_row
        own_start = (col * n_row + row) * span

        def pad_rows(value):
            return jnp.pad(value, ((0, padded - value.shape[0]), (0, 0)))

        def dp_join(value):
            other = dp_swap(value)
            low = jnp.where(rank == 0, value, other)
            high = jnp.where(rank == 0, other, value)
            return low, high

        def dp_half(value, axis):
            size = value.shape[axis] // 2
            return lax.dynamic_slice_in_dim(value, rank * size, size, axis)

        def own_rows(value):
            return lax.dynamic_slice_in_dim(value, own_start, span, 0)

        def gather_tokens(value):
            mine = lax.dynamic_slice_in_dim(pad_rows(value), col * block, block, 0)
            pieces = row_all(mine)
            return pieces, lambda: col_all(jnp.concatenate(pieces, axis=1), col).reshape(
                padded, width
            )

        def weight_move(value, parts):
            wide = value.reshape(value.shape[0], n_row, parts).transpose(1, 0, 2)
            if paired:
                wide = dp_half(wide, 1)
            return wide

        def weight_swap(wide):
            return [row_shift(pick(wide, (row + k) % n_row), k) for k in range(n_row)]

        def weight_join(pieces):
            moved = jnp.stack(pieces)
            if paired:
                moved = jnp.concatenate(dp_join(moved), axis=1)
            return moved.reshape(-1, moved.shape[-1])

        def grad_sum(blocks):
            low = blocks.astype(LOW)
            if paired:
                size = low.shape[1] // 2
                kept = dp_half(low, 1)
                sent = lax.dynamic_slice_in_dim(low, (1 - rank) * size, size, 1)
                low = (kept.astype(WIDE) + dp_swap(sent).astype(WIDE)).astype(LOW)
            elif n_dp > 1:
                low = lax.psum(blocks, "dp").astype(LOW)
            pieces = [row_shift(low[(-k) % n_row], k) for k in range(n_row)]
            joined = row_place(pieces, row)
            if paired:
                joined = jnp.concatenate(dp_join(joined), axis=1)
            return joined

        def sum_rows(product, rows):
            held = rows.reshape((2,) * len(masks) + (block,) + rows.shape[1:])
            axis = len(masks) - 1
            bit = (col >> 0) & 1
            sent = product(pick(held, 1 - bit, axis).reshape(-1, rows.shape[1])).astype(LOW)
            got = col_swap(sent, 1)
            kept = product(pick(held, bit, axis).reshape(-1, rows.shape[1]))
            total = kept + got.astype(WIDE)
            for stage, mask in enumerate(masks[1:], 1):
                left = len(masks) - stage
                total = total.reshape((2,) * left + (block, width))
                bit = (col >> stage) & 1
                sent = pick(total, 1 - bit, left - 1).astype(LOW)
                got = col_swap(sent, mask)
                total = pick(total, bit, left - 1) + got.astype(WIDE)
            total = total.reshape(n_row, span, width)
            result = pick(total, row)
            for k in range(1, n_row):
                got = row_shift(pick(total, (row + k) % n_row).astype(LOW), k)
                result = result + roll_blocks(got.astype(WIDE), k)
            return result

        def spread_rows(rows):
            low = rows.astype(LOW)
            pieces = [roll_blocks(row_shift(low, k), k) for k in range(n_row)]
            return col_all(row_place(pieces, row), col).reshape(padded, width)

        def spread_feats(rows):
            low = rows.astype(LOW)
            pieces = []
            for k in range(n_row):
                j = (-k) % n_row
                pieces.append(row_shift(low[:, j * feats : (j + 1) * feats], k))
            return col_all(row_place(pieces, row), col).reshape(padded, feats)[:tokens]

        small = jnp.stack([pre_gain, pre_shift, merge_bias, mid_gain, mid_shift, reduce_bias])
        small = jnp.concatenate(row_all(small), axis=1)
        gain1, shift1, bias1, gain2, shift2, bias2 = [small[i : i + 1] for i in range(6)]
        x_pieces, x_finish = gather_tokens(inputs)
        joint_wide = weight_move(joint_weight, trio)
        joint_pieces = weight_swap(joint_wide)
        x_full = x_finish()
        joint_own = weight_join(joint_pieces)

        merge_low, cot_low = lax.optimization_barrier(
            (merge_weight, cotangent, x_pieces[-1], joint_pieces[-1])
        )[:2]
        merge_half = dp_half(merge_low, 0) if paired else merge_low
        merge_rows = jnp.concatenate(row_all(merge_half), axis=1)
        cot_pieces, cot_finish = gather_tokens(cot_low)
        merge_rows = jnp.concatenate(dp_join(merge_rows), axis=0) if paired else merge_rows
        merge_full = col_all(merge_rows, col).reshape(width, width)
        mlp_wide = jnp.concatenate(
            [weight_move(expand_weight, units), weight_move(reduce_weight.T, units)], axis=2
        )
        mlp_wide = after(mlp_wide, merge_rows)
        mlp_own = weight_join(weight_swap(mlp_wide))
        expand_own = mlp_own[:, :units]
        reduce_own = mlp_own[:, units:]
        cot_full = cot_finish()

        residual = x_full.astype(WIDE)
        unit1, inv1 = norm_forward(residual)
        normed1 = (unit1 * gain1 + shift1).astype(LOW)
        own_bias = joint_bias.reshape(2 * head_size)
        bias_row = jnp.concatenate(
            [own_bias[:head_size], jnp.zeros((head_size,), WIDE), own_bias[head_size:]]
        )
        joint_rows = (dot(normed1, joint_own, 1, 0) + bias_row).astype(LOW)[:tokens]
        per_image = joint_rows.reshape(images, SEQ, 3 * head_size)
        query_rows = per_image[..., :head_size]
        key_rows = per_image[..., head_size : 2 * head_size]
        value_rows = per_image[..., 2 * head_size :]
        context, totals = attend(query_rows, key_rows, value_rows)

        own_context = pad_rows(context.reshape(tokens, head_size)).T
        context_all = col_all(row_place(row_all(own_context), row), col)
        context_full = context_all.reshape(width, padded)
        mixed1 = residual + dot(context_full, merge_full, 0, 0) + bias1
        unit2, inv2 = norm_forward(mixed1)
        normed2 = (unit2 * gain2 + shift2).astype(LOW)

        own_units = lax.dynamic_slice_in_dim(expand_bias, row * units, units, 0)
        hidden_pre = dot(normed2, expand_own, 1, 0) + own_units
        value, slope = gelu_pair(hidden_pre)
        active = value.astype(LOW)
        hidden_grad = (dot(cot_full, reduce_own, 1, 0) * slope).astype(LOW)
        normed2_grad = sum_rows(lambda rows: dot(rows, expand_own, 1, 1), hidden_grad)

        unit2_own = own_rows(unit2)
        cot_own = own_rows(cot_full).astype(WIDE)
        mixed_grad = cot_own + norm_backward(normed2_grad, unit2_own, own_rows(inv2), gain2)
        mixed_low = spread_rows(mixed_grad)

        out_rows = sum_rows(lambda rows: dot(rows, reduce_own, 1, 1), after(active, mixed_low))
        outputs = spread_feats(own_rows(mixed1) + out_rows + bias2)

        expand_grad = dot(normed2, hidden_grad, 0, 0).reshape(n_row, feats, units)
        reduce_grad = dot(cot_full, active, 0, 0).reshape(n_row, feats, units)
        mlp_grad = grad_sum(jnp.concatenate([expand_grad, reduce_grad], axis=2))
        expand_weight_grad = (
            mlp_grad[..., :units].transpose(1, 0, 2).reshape(feats, -1).astype(WIDE)
        )
        reduce_weight_grad = (
            mlp_grad[..., units:].transpose(0, 2, 1).reshape(-1, feats).astype(WIDE)
        )

        head_rows = lax.dynamic_slice_in_dim(
            merge_full, (col * n_row + row) * head_size, head_size, 0
        )
        context_grad = dot(mixed_low, head_rows, 1, 1).astype(LOW)[:tokens]
        query_grad, key_grad, value_grad = attend_back(
            query_rows,
            key_rows,
            value_rows,
            context,
            totals,
            context_grad.reshape(images, SEQ, head_size),
        )
        joint_grad = jnp.concatenate([query_grad, key_grad, value_grad], axis=-1)
        joint_grad = pad_rows(joint_grad.reshape(tokens, 3 * head_size).astype(LOW))
        joint_bias_grad = jnp.concatenate(
            [jnp.sum(query_grad, axis=(0, 1)), jnp.sum(value_grad, axis=(0, 1))]
        )
        normed1_grad = sum_rows(lambda rows: dot(rows, joint_own, 1, 1), joint_grad)
        unit1_own = own_rows(unit1)
        inputs_rows = mixed_grad + norm_backward(normed1_grad, unit1_own, own_rows(inv1), gain1)
        inputs_grad = spread_feats(inputs_rows).astype(WIDE)

        joint_blocks = grad_sum(dot(normed1, joint_grad, 0, 0).reshape(n_row, feats, trio))
        joint_weight_grad = joint_blocks.transpose(1, 0, 2).reshape(feats, -1).astype(WIDE)
        group_context = pick(context_all.reshape(n_col, n_row * head_size, padded), col)
        merge_weight_grad = dot(group_context, mixed_low[:, :feats], 1, 0)
        if paired:
            merge_grad_low = merge_weight_grad.astype(LOW)
            merge_weight_grad = merge_grad_low.astype(WIDE) + dp_swap(merge_grad_low).astype(WIDE)
        else:
            merge_weight_grad = dp_sum(merge_weight_grad)

        sums = jnp.stack(
            [
                jnp.sum(normed2_grad * unit2_own, axis=0),
                jnp.sum(normed2_grad, axis=0),
                jnp.sum(mixed_grad, axis=0),
                jnp.sum(normed1_grad * unit1_own, axis=0),
                jnp.sum(normed1_grad, axis=0),
            ]
        )
        for mask in masks:
            sums = sums + col_swap(sums, mask)
        pieces = []
        for k in range(n_row):
            j = (-k) % n_row
            pieces.append(row_shift(sums[:, j * feats : (j + 1) * feats], k))
        stacked = row_place(pieces, row)
        sums = dp_sum(jnp.sum(stacked, axis=0))
        mid_gain_grad, mid_shift_grad, merge_bias_grad, pre_gain_grad, pre_shift_grad = [
            sums[i] for i in range(5)
        ]
        local = jnp.concatenate(
            [jnp.sum(hidden_grad, axis=0, dtype=WIDE), joint_bias_grad]
        )
        local = dp_sum(local)
        joint_bias_grad = local[units:].reshape(joint_bias.shape)
        expand_bias_grad = row_place(row_all(local[:units]), row).reshape(-1)
        reduce_bias_grad = dp_sum(jnp.sum(cotangent.astype(WIDE), axis=0))
        return (
            outputs,
            inputs_grad,
            pre_gain_grad,
            pre_shift_grad,
            joint_weight_grad,
            joint_bias_grad,
            merge_weight_grad,
            merge_bias_grad,
            mid_gain_grad,
            mid_shift_grad,
            expand_weight_grad,
            expand_bias_grad,
            reduce_weight_grad,
            reduce_bias_grad,
        )

    return body


def solution(mesh):
    in_specs = (
        P("dp", "row"),
        P("row"),
        P("row"),
        P("row", "col"),
        P("col", "row", None),
        P("col", "row"),
        P("row"),
        P("row"),
        P("row"),
        P("row", "col"),
        P("col"),
        P("col", "row"),
        P("row"),
        P("dp", "row"),
    )
    out_specs = (
        P("dp", "row"),
        P("dp", "row"),
        P("row"),
        P("row"),
        P("row", "col"),
        P("col", "row", None),
        P("col", "row"),
        P("row"),
        P("row"),
        P("row"),
        P("row", "col"),
        P("col"),
        P("col", "row"),
        P("row"),
    )
    body = make_body(mesh.shape["dp"], mesh.shape["row"], mesh.shape["col"])
    return jax.shard_map(body, mesh=mesh, in_specs=in_specs, out_specs=out_specs, check_vma=False)
```

```python
import jax
import jax.numpy as jnp
from jax import lax
from jax.experimental.layout import Layout, with_layout_constraint
from jax.sharding import PartitionSpec as P

D = 1152
SEQ = 729


NORM_EPSILON = 1e-06
TANH_SLOPE = 0.7978845608028654
CUBIC_TERM = 0.044715
LOW = jnp.bfloat16
WIDE = jnp.float32


def gelu_pair(preact):
    inner_tanh = jnp.tanh(TANH_SLOPE * (preact + CUBIC_TERM * preact * preact * preact))
    value = 0.5 * preact * (1.0 + inner_tanh)
    slope = 0.5 * (1.0 + inner_tanh) + 0.5 * preact * (
        1.0 - inner_tanh * inner_tanh
    ) * TANH_SLOPE * (1.0 + 3.0 * CUBIC_TERM * preact * preact)
    return value, slope


def dot(left, right, left_dim, right_dim):
    return lax.dot_general(
        left, right, (((left_dim,), (right_dim,)), ((), ())), preferred_element_type=WIDE
    )


def pick(blocks, index, axis=0):
    return lax.dynamic_index_in_dim(blocks, index, axis, keepdims=False)


def place(blocks, block, index):
    return lax.dynamic_update_index_in_dim(blocks, block, index, 0)


def after(values, *others):
    return lax.optimization_barrier((values,) + others)[0]


def straight(values):
    return with_layout_constraint(values, Layout(tuple(range(values.ndim))))


def norm_forward(values):
    row_mean = jnp.mean(values, axis=-1, keepdims=True)
    row_var = jnp.mean(values * values, axis=-1, keepdims=True) - row_mean * row_mean
    inv_scale = lax.rsqrt(row_var + NORM_EPSILON)
    return (values - row_mean) * inv_scale, inv_scale


def norm_backward(upstream, unit_rows, inv_scale, norm_gain):
    scaled = upstream * norm_gain
    first = jnp.mean(scaled, axis=-1, keepdims=True)
    second = jnp.mean(scaled * unit_rows, axis=-1, keepdims=True)
    return inv_scale * (scaled - first - unit_rows * second)


def attend(query_rows, key_rows, value_rows, factor, keep):
    scores = dot(query_rows, key_rows, 1, 1) * factor
    totals = jnp.log(jnp.sum(jnp.exp(scores) * keep, axis=-1, keepdims=True))
    softmax_rows = (jnp.exp(scores - totals) * keep).astype(LOW)
    return dot(value_rows, softmax_rows, 0, 1).astype(LOW), totals


def attend_back(query_rows, key_rows, value_rows, context, totals, upstream, factor, keep):
    scores = dot(query_rows, key_rows, 1, 1) * factor
    weights = jnp.exp(scores - totals) * keep
    value_grad = dot(weights.astype(LOW), upstream, 0, 0)
    prob_grad = dot(upstream, value_rows, 1, 1)
    row_delta = jnp.sum(
        upstream.astype(WIDE) * context.T.astype(WIDE), axis=-1, keepdims=True
    )
    score_grad = (weights * (prob_grad - row_delta)).astype(LOW)
    scale = query_rows.shape[-1] ** (-0.5)
    query_grad = dot(score_grad, key_rows, 1, 0) * scale
    key_grad = dot(score_grad, query_rows, 0, 0) * scale
    return query_grad, key_grad, value_grad


def split_wide(value):
    high = value.astype(LOW)
    rest = value - high.astype(WIDE)
    middle = rest.astype(LOW)
    last = (rest - middle.astype(WIDE)).astype(LOW)
    return jnp.concatenate([high, middle, last], axis=0)


def merge_wide(rows):
    high, middle, last = jnp.split(rows.astype(WIDE), 3, axis=-2)
    return high + (middle + last)


def make_body(n_dp, n_row, n_col):
    masks = []
    while (1 << len(masks)) < n_col:
        masks.append(1 << len(masks))
    paired = n_dp == 2

    def col_swap(value, mask):
        return lax.ppermute(value, "col", [(i, i ^ mask) for i in range(n_col)])

    def dp_swap(value):
        return lax.ppermute(value, "dp", [(0, 1), (1, 0)])

    def row_exchange(blocks):
        return lax.all_to_all(blocks, "row", 0, 0, tiled=True)

    def row_gather(value):
        return row_exchange(jnp.broadcast_to(value[None], (n_row,) + value.shape))

    def col_parts(value):
        parts = [value]
        for mask in reversed(masks):
            parts = parts + [col_swap(part, mask) for part in parts]
        return parts

    def align_lanes(part, offset, near):
        size = part.shape[1] // n_col
        source = [near.index(mine ^ offset) for mine in near]
        return jnp.concatenate([part[:, i * size : (i + 1) * size] for i in source], axis=1)

    def col_gather(value):
        return jnp.concatenate(col_parts(value), axis=0)

    def body(
        inputs,
        pre_gain,
        pre_shift,
        joint_weight,
        joint_bias,
        merge_weight,
        merge_bias,
        mid_gain,
        mid_shift,
        expand_weight,
        expand_bias,
        reduce_weight,
        reduce_bias,
        cotangent,
    ):
        row = lax.axis_index("row")
        col = lax.axis_index("col")
        rank = lax.axis_index("dp")
        near = [0]
        for mask in reversed(masks):
            near = near + [offset ^ mask for offset in near]
        tokens, feats = inputs.shape
        width = feats * n_row
        images = tokens // SEQ
        head_size = joint_bias.shape[2] // 2
        span = -(-tokens // (n_row * n_col * 16)) * 16
        padded = span * n_row * n_col
        block = span * n_row
        units = expand_weight.shape[1] // n_row
        trio = joint_weight.shape[1] // n_row

        def pad_rows(value):
            return jnp.pad(value, ((0, padded - value.shape[0]), (0, 0)))

        def join(value, other, bit, axis):
            low = jnp.where(bit == 0, value, other)
            high = jnp.where(bit == 0, other, value)
            return straight(jnp.concatenate([low, high], axis=axis))

        def half_of(value, index, axis):
            size = value.shape[axis] // 2
            return lax.dynamic_slice_in_dim(value, index * size, size, axis)

        def own_rows(value):
            return lax.dynamic_slice_in_dim(value, row * span, span, 0)

        def own_block(value):
            return lax.dynamic_slice_in_dim(pad_rows(value), col * block, block, 0)

        def everywhere(value):
            return [value] * n_row

        def fit_lanes(blocks):
            return [jnp.pad(b, ((0, 0), (0, feats - b.shape[1]))) for b in blocks]

        def pack(*pieces):
            return straight(jnp.stack([jnp.concatenate(group, axis=0) for group in zip(*pieces)]))

        def height(piece):
            return piece[0].shape[0]

        def lanes(blocks):
            return jnp.concatenate([blocks[i] for i in range(n_row)], axis=-1)

        def weight_move(value, parts):
            mine = half_of(value, rank, 0) if paired else value
            return [mine[:, j * parts : (j + 1) * parts] for j in range(n_row)]

        def weight_move_rows(value, parts):
            mine = half_of(value, rank, 1) if paired else value
            return [mine[j * parts : (j + 1) * parts].T for j in range(n_row)]

        def weight_join(moved):
            if paired:
                moved = join(moved, dp_swap(moved), rank, 1)
            return moved.reshape(-1, moved.shape[-1])

        def grad_start(blocks):
            low = blocks.astype(LOW)
            if paired:
                sent = half_of(low, 1 - rank, 1)
                kept = half_of(low, rank, 1)
                low = (kept.astype(WIDE) + dp_swap(sent).astype(WIDE)).astype(LOW)
            elif n_dp > 1:
                low = lax.psum(blocks.astype(WIDE), "dp").astype(LOW)
            return low

        def grad_join(moved):
            return join(moved, dp_swap(moved), rank, 1) if paired else moved

        def sum_rows(product, rows, late=None):
            size = padded // 2
            got = col_swap(product(rows[size:]).astype(LOW), masks[0])
            total = product(rows[:size]) + got.astype(WIDE)
            for mask in masks[1:]:
                size //= 2
                total = total[:size] + col_swap(total[size:].astype(LOW), mask).astype(WIDE)
            total = total.astype(LOW)
            if late is not None:
                total = after(total, late)
            parts = row_exchange(total.reshape(n_row, span, width))
            return jnp.sum(parts.astype(WIDE), axis=0)

        def feature_blocks(rows):
            return [rows[:, j * feats : (j + 1) * feats] for j in range(n_row)]

        small = split_wide(
            jnp.stack([pre_gain, pre_shift, merge_bias, mid_gain, mid_shift, reduce_bias])
        )
        joint_wide = weight_move(joint_weight, trio)
        first = row_exchange(
            pack(everywhere(own_block(inputs)), everywhere(small), fit_lanes(joint_wide))
        )
        pieces = [
            everywhere(own_block(cotangent)),
            everywhere(half_of(merge_weight, rank, 0) if paired else merge_weight),
            fit_lanes(weight_move(expand_weight, units)),
            fit_lanes(weight_move_rows(reduce_weight, units)),
        ]
        second = row_exchange(after(pack(*pieces), first))
        ends = [sum(height(piece) for piece in pieces[:i]) for i in range(5)]
        cot_moved, merge_moved, expand_moved, reduce_moved = [
            second[:, low:high] for low, high in zip(ends, ends[1:])
        ]
        inner = block + small.shape[0]
        small_full = merge_wide(lanes(first[:, block:inner]))
        gain1, shift1, bias1, gain2, shift2, bias2 = [small_full[i : i + 1] for i in range(6)]
        x_full = col_gather(lanes(first[:, :block]))
        joint_own = weight_join(first[:, inner:, :trio])

        residual = x_full.astype(WIDE)
        unit1, inv1 = norm_forward(residual)
        normed1 = (unit1 * gain1 + shift1).astype(LOW)
        own_bias = joint_bias.reshape(2 * head_size)
        bias_row = jnp.concatenate(
            [own_bias[:head_size], jnp.zeros((head_size,), WIDE), own_bias[head_size:]]
        )
        joint_rows = (dot(normed1, joint_own, 1, 0) + bias_row).astype(LOW)
        query_rows = joint_rows[:, :head_size]
        key_rows = joint_rows[:, head_size : 2 * head_size]
        value_rows = joint_rows[:, 2 * head_size :]
        order = jnp.concatenate([(col ^ offset) * block + jnp.arange(block) for offset in near])
        real = (order < tokens).astype(WIDE)
        factor = real[:, None] * head_size ** (-0.5)
        keep = real[None]
        if images > 1:
            keep = keep * (order[:, None] // SEQ == order[None] // SEQ).astype(WIDE)
        own_context, totals = attend(query_rows, key_rows, value_rows, factor, keep)

        cot_full = col_gather(lanes(cot_moved))
        merge_rows = lanes(merge_moved)
        if paired:
            merge_rows = join(merge_rows, dp_swap(merge_rows), rank, 0)
        merge_full = col_gather(merge_rows)
        expand_own = weight_join(expand_moved[..., :units])
        reduce_own = weight_join(reduce_moved[..., :units])

        group_context = row_gather(after(own_context, second)).reshape(n_row * head_size, padded)
        context_full = jnp.concatenate(
            [
                align_lanes(part, offset, near) if offset else part
                for part, offset in zip(col_parts(group_context), near)
            ],
            axis=0,
        )
        mixed1 = residual + dot(context_full, merge_full, 0, 0) + bias1
        unit2, inv2 = norm_forward(mixed1)
        normed2 = (unit2 * gain2 + shift2).astype(LOW)

        own_units = lax.dynamic_slice_in_dim(expand_bias, row * units, units, 0)
        hidden_pre = dot(normed2, expand_own, 1, 0) + own_units
        value, slope = gelu_pair(hidden_pre)
        active = value.astype(LOW)
        hidden_grad = (dot(cot_full, reduce_own, 1, 0) * slope).astype(LOW)
        normed2_grad = sum_rows(lambda rows: dot(rows, expand_own, 1, 1), hidden_grad)

        unit2_own = own_rows(unit2)
        cot_own = own_rows(cot_full).astype(WIDE)
        mixed_grad = cot_own + norm_backward(normed2_grad, unit2_own, own_rows(inv2), gain2)
        mixed_block = row_gather(mixed_grad.astype(LOW)).reshape(block, width)
        mixed_low = col_gather(mixed_block)
        out_rows = sum_rows(
            lambda rows: dot(rows, reduce_own, 1, 1), after(active, normed2_grad), mixed_block
        )
        out_rows = (own_rows(mixed1) + out_rows + bias2).astype(LOW)

        expand_grad = dot(normed2, hidden_grad, 0, 0).reshape(n_row, feats, units)
        reduce_grad = dot(cot_full, active, 0, 0).reshape(n_row, feats, units)
        mlp_grad = grad_start(
            jnp.concatenate([expand_grad.astype(LOW), reduce_grad.astype(LOW)], axis=2)
        )
        mlp_grad = grad_join(row_exchange(after(mlp_grad, out_rows)))
        expand_weight_grad = (
            lanes(mlp_grad[..., :units]).astype(WIDE)
        )
        reduce_weight_grad = (
            jnp.concatenate([mlp_grad[j, :, units:].T for j in range(n_row)]).astype(WIDE)
        )

        head_rows = lax.dynamic_slice_in_dim(merge_full, row * head_size, head_size, 0)
        context_grad = dot(mixed_low, head_rows, 1, 1).astype(LOW)
        query_grad, key_grad, value_grad = attend_back(
            query_rows, key_rows, value_rows, own_context, totals, context_grad, factor, keep
        )
        joint_grad = jnp.concatenate([query_grad, key_grad, value_grad], axis=-1).astype(LOW)
        joint_bias_grad = jnp.concatenate(
            [jnp.sum(query_grad, axis=0), jnp.sum(value_grad, axis=0)]
        )
        normed1_grad = sum_rows(lambda rows: dot(rows, joint_own, 1, 1), joint_grad)
        unit1_own = own_rows(unit1)
        inputs_rows = mixed_grad + norm_backward(normed1_grad, unit1_own, own_rows(inv1), gain1)

        joint_blocks = grad_start(dot(normed1, joint_grad, 0, 0).reshape(n_row, feats, trio))
        own_mixed = lax.dynamic_slice_in_dim(mixed_low, row * feats, feats, 1)
        merge_weight_grad = dot(group_context, own_mixed, 1, 0)
        if paired:
            merge_grad_low = merge_weight_grad.astype(LOW)
            merge_weight_grad = merge_grad_low.astype(WIDE) + dp_swap(merge_grad_low).astype(WIDE)
        elif n_dp > 1:
            merge_weight_grad = lax.psum(merge_weight_grad, "dp")

        sums = jnp.stack(
            [
                jnp.sum(normed2_grad * unit2_own, axis=0),
                jnp.sum(normed2_grad, axis=0),
                jnp.sum(mixed_grad, axis=0),
                jnp.sum(normed1_grad * unit1_own, axis=0),
                jnp.sum(normed1_grad, axis=0),
            ]
        )
        hidden_sum = jnp.pad(
            jnp.sum(hidden_grad, axis=0, dtype=WIDE), (0, -(-units // feats) * feats - units)
        ).reshape(-1, feats)
        hidden_rows = hidden_sum.shape[0]
        hidden_low = split_wide(hidden_sum)
        sums_low = [jnp.concatenate([p, hidden_low]) for p in feature_blocks(split_wide(sums))]
        final = row_exchange(
            pack(
                feature_blocks(out_rows),
                feature_blocks(inputs_rows.astype(LOW)),
                sums_low,
                fit_lanes([joint_blocks[j] for j in range(n_row)]),
            )
        )
        ends = 2 * span + height(sums_low)
        vectors = final[:, 2 * span : ends]
        joint_blocks = grad_join(final[:, ends:, :trio])
        joint_weight_grad = lanes(joint_blocks).astype(WIDE)
        partial = jnp.sum(merge_wide(vectors[:, :15]), axis=0)
        hidden_all = merge_wide(vectors[:, 15:]).reshape(n_row, -1)[:, :units].reshape(-1)
        local = jnp.concatenate([hidden_all, joint_bias_grad])
        local = jnp.pad(local, (0, -local.shape[0] % feats)).reshape(-1, feats)
        local = jnp.concatenate(
            [partial, jnp.sum(cotangent.astype(WIDE), axis=0)[None], local], axis=0
        )
        shared = lax.all_gather(
            jnp.concatenate(
                [final[:, : 2 * span].reshape(2 * block, feats), split_wide(local)], axis=0
            ),
            "col",
        )
        spread = shared[:, : 2 * block].reshape(n_col, n_row, 2 * span, feats)
        outputs = spread[:, :, :span].reshape(padded, feats)[:tokens]
        inputs_grad = spread[:, :, span:].reshape(padded, feats)[:tokens].astype(WIDE)
        shared = merge_wide(shared[:, 2 * block :])
        vector_sums = jnp.concatenate([jnp.sum(shared[:, :5], axis=0), pick(shared, col)[5:]])
        if paired:
            vector_sums = vector_sums + dp_swap(vector_sums)
        elif n_dp > 1:
            vector_sums = lax.psum(vector_sums, "dp")
        reduce_bias_grad = vector_sums[5]
        own_sums = vector_sums[6:].reshape(-1)
        mid_gain_grad, mid_shift_grad, merge_bias_grad, pre_gain_grad, pre_shift_grad = [
            vector_sums[i] for i in range(5)
        ]
        tail = n_row * units
        expand_bias_grad = own_sums[:tail]
        joint_bias_grad = own_sums[tail : tail + 2 * head_size].reshape(joint_bias.shape)
        return (
            outputs,
            inputs_grad,
            pre_gain_grad,
            pre_shift_grad,
            joint_weight_grad,
            joint_bias_grad,
            merge_weight_grad,
            merge_bias_grad,
            mid_gain_grad,
            mid_shift_grad,
            expand_weight_grad,
            expand_bias_grad,
            reduce_weight_grad,
            reduce_bias_grad,
        )

    return body


def solution(mesh):
    in_specs = (
        P("dp", "row"),
        P("row"),
        P("row"),
        P("row", "col"),
        P("col", "row", None),
        P("col", "row"),
        P("row"),
        P("row"),
        P("row"),
        P("row", "col"),
        P("col"),
        P("col", "row"),
        P("row"),
        P("dp", "row"),
    )
    out_specs = (
        P("dp", "row"),
        P("dp", "row"),
        P("row"),
        P("row"),
        P("row", "col"),
        P("col", "row", None),
        P("col", "row"),
        P("row"),
        P("row"),
        P("row"),
        P("row", "col"),
        P("col"),
        P("col", "row"),
        P("row"),
    )
    body = make_body(mesh.shape["dp"], mesh.shape["row"], mesh.shape["col"])
    return jax.shard_map(body, mesh=mesh, in_specs=in_specs, out_specs=out_specs, check_vma=False)
```

```python
import jax
import jax.numpy as jnp
from jax import lax
from jax.experimental import pallas as pl
from jax.experimental.layout import Layout, with_layout_constraint
from jax.experimental.pallas import tpu as pltpu
from jax.sharding import PartitionSpec as P

D = 1152
SEQ = 729


NORM_EPSILON = 1e-06
TANH_SLOPE = 0.7978845608028654
CUBIC_TERM = 0.044715
LOW = jnp.bfloat16
WIDE = jnp.float32


def gelu_pair(preact):
    inner_tanh = jnp.tanh(TANH_SLOPE * (preact + CUBIC_TERM * preact * preact * preact))
    value = 0.5 * preact * (1.0 + inner_tanh)
    slope = 0.5 * (1.0 + inner_tanh) + 0.5 * preact * (
        1.0 - inner_tanh * inner_tanh
    ) * TANH_SLOPE * (1.0 + 3.0 * CUBIC_TERM * preact * preact)
    return value, slope


def dot(left, right, left_dim, right_dim):
    return lax.dot_general(
        left, right, (((left_dim,), (right_dim,)), ((), ())), preferred_element_type=WIDE
    )


def pick(blocks, index, axis=0):
    return lax.dynamic_index_in_dim(blocks, index, axis, keepdims=False)


def place(blocks, block, index):
    return lax.dynamic_update_index_in_dim(blocks, block, index, 0)


def after(values, *others):
    return lax.optimization_barrier((values,) + others)[0]


def straight(values):
    return with_layout_constraint(values, Layout(tuple(range(values.ndim))))


def norm_forward(values):
    row_mean = jnp.mean(values, axis=-1, keepdims=True)
    row_var = jnp.mean(values * values, axis=-1, keepdims=True) - row_mean * row_mean
    inv_scale = lax.rsqrt(row_var + NORM_EPSILON)
    return (values - row_mean) * inv_scale, inv_scale


def norm_backward(upstream, unit_rows, inv_scale, norm_gain):
    scaled = upstream * norm_gain
    first = jnp.mean(scaled, axis=-1, keepdims=True)
    second = jnp.mean(scaled * unit_rows, axis=-1, keepdims=True)
    return inv_scale * (scaled - first - unit_rows * second)


def attend(query_rows, key_rows, value_rows, factor, keep):
    scores = dot(query_rows, key_rows, 1, 1) * factor
    totals = jnp.log(jnp.sum(jnp.exp(scores) * keep, axis=-1, keepdims=True))
    softmax_rows = (jnp.exp(scores - totals) * keep).astype(LOW)
    return dot(value_rows, softmax_rows, 0, 1).astype(LOW), totals


def attend_back(query_rows, key_rows, value_rows, context, totals, upstream, factor, keep):
    scores = dot(query_rows, key_rows, 1, 1) * factor
    weights = jnp.exp(scores - totals) * keep
    value_grad = dot(weights.astype(LOW), upstream, 0, 0)
    prob_grad = dot(upstream, value_rows, 1, 1)
    row_delta = jnp.sum(
        upstream.astype(WIDE) * context.T.astype(WIDE), axis=-1, keepdims=True
    )
    score_grad = (weights * (prob_grad - row_delta)).astype(LOW)
    scale = query_rows.shape[-1] ** (-0.5)
    query_grad = dot(score_grad, key_rows, 1, 0) * scale
    key_grad = dot(score_grad, query_rows, 0, 0) * scale
    return query_grad, key_grad, value_grad


def split_wide(value):
    high = lax.reduce_precision(value, 8, 7)
    rest = value - high
    middle = lax.reduce_precision(rest, 8, 7)
    return jnp.concatenate([high, middle, rest - middle], axis=0).astype(LOW)


def merge_wide(rows):
    high, middle, last = jnp.split(rows.astype(WIDE), 3, axis=-2)
    return high + (middle + last)


def local_call(kernel, outs, scalars, *arrays, scratch=()):
    return pl.pallas_call(
        kernel,
        out_shape=[jax.ShapeDtypeStruct(shape, kind) for shape, kind in outs],
        grid_spec=pltpu.PrefetchScalarGridSpec(
            num_scalar_prefetch=1,
            grid=(1,),
            in_specs=[
                pl.BlockSpec(a.shape, lambda i, _, n=a.ndim: (0,) * n) for a in arrays
            ],
            out_specs=[
                pl.BlockSpec(shape, lambda i, _, n=len(shape): (0,) * n) for shape, _ in outs
            ],
            scratch_shapes=list(scratch),
        ),
    )(scalars, *arrays)


def split_blocks(moved, plan):
    sources = moved.shape[0]
    outs = []
    for _, rows, used, side in plan:
        shape = (rows, sources * used) if side else (sources * rows, used)
        outs.append((shape, moved.dtype))

    def kernel(_, moved_ref, *out_refs):
        for (start, rows, used, side), out_ref in zip(plan, out_refs):
            for i in range(sources):
                piece = moved_ref[i, start : start + rows, :used]
                if side:
                    out_ref[:, i * used : (i + 1) * used] = piece
                else:
                    out_ref[i * rows : (i + 1) * rows, :] = piece

    return local_call(kernel, outs, jnp.zeros((1,), jnp.int32), moved)


def pack_first(inputs, joint_weight, vectors, col, rank, block, padded, parts, halves):
    tokens, feats = inputs.shape
    count = len(vectors)
    small = -(-3 * count // 16) * 16
    half = feats // halves
    rows = block + small + half

    def kernel(place_ref, input_ref, joint_ref, *refs):
        vector_refs, (out_ref, wide_ref, token_ref) = refs[:count], refs[count:]
        token_ref[...] = jnp.zeros_like(token_ref)
        token_ref[:tokens, :] = input_ref[...]
        wide_ref[...] = jnp.zeros_like(wide_ref)
        for i, vector_ref in enumerate(vector_refs):
            value = vector_ref[...].reshape(1, feats)
            high = value.astype(LOW).astype(WIDE)
            middle = (value - high).astype(LOW).astype(WIDE)
            wide_ref[i : i + 1, :] = high
            wide_ref[count + i : count + i + 1, :] = middle
            wide_ref[2 * count + i : 2 * count + i + 1, :] = value - high - middle
        start = pl.multiple_of(place_ref[0] * block, 16)
        mine = token_ref[pl.ds(start, block), :]
        low = wide_ref[...].astype(LOW)
        joint = joint_ref[pl.ds(pl.multiple_of(place_ref[1] * half, 16), half), :]
        for j in range(out_ref.shape[0]):
            out_ref[j, :block, :] = mine
            out_ref[j, block : block + small, :] = low
            out_ref[j, block + small :, :parts] = joint[:, j * parts : (j + 1) * parts]
            out_ref[j, block + small :, parts:] = jnp.zeros((half, feats - parts), LOW)

    count_out = joint_weight.shape[1] // parts
    place_at = jnp.stack([col, rank if halves == 2 else 0 * rank]).astype(jnp.int32)
    return local_call(
        kernel,
        [((count_out, rows, feats), LOW)],
        place_at,
        inputs,
        joint_weight,
        *vectors,
        scratch=(pltpu.VMEM((small, feats), WIDE), pltpu.VMEM((padded, feats), LOW)),
    )[0]


def join_halves(mine, other, rank, groups):
    rows = mine.shape[0] // groups
    outs = [((2 * mine.shape[0], mine.shape[1]), mine.dtype)]

    def kernel(rank_ref, mine_ref, other_ref, out_ref):
        for i in range(groups):
            first = pl.multiple_of((2 * i + rank_ref[0]) * rows, 16)
            second = pl.multiple_of((2 * i + 1 - rank_ref[0]) * rows, 16)
            out_ref[pl.ds(first, rows), :] = mine_ref[i * rows : (i + 1) * rows, :]
            out_ref[pl.ds(second, rows), :] = other_ref[i * rows : (i + 1) * rows, :]

    return local_call(kernel, outs, rank.reshape(1).astype(jnp.int32), mine, other)[0]


def mlp_blocks(moved, rows, used):
    sources = moved.shape[0]

    def kernel(_, moved_ref, out_ref):
        for i in range(sources):
            at = slice(i * rows, (i + 1) * rows)
            out_ref[at, :used] = moved_ref[i, :rows, :used]
            out_ref[at, used : 2 * used] = moved_ref[i, rows:, :used]
            out_ref[at, 2 * used :] = jnp.zeros((rows, out_ref.shape[1] - 2 * used), LOW)

    outs = [((sources * rows, -(-2 * used // 128) * 128), moved.dtype)]
    return local_call(kernel, outs, jnp.zeros((1,), jnp.int32), moved)[0]


def mlp_join(mine, other, rank, groups, used, paired):
    if not paired:
        return mine[:, :used], mine[:, used : 2 * used]
    rows = mine.shape[0] // groups

    def kernel(rank_ref, mine_ref, other_ref, *out_refs):
        for i in range(groups):
            at = slice(i * rows, (i + 1) * rows)
            first = pl.multiple_of((2 * i + rank_ref[0]) * rows, 16)
            second = pl.multiple_of((2 * i + 1 - rank_ref[0]) * rows, 16)
            for k, out_ref in enumerate(out_refs):
                lanes = slice(k * used, (k + 1) * used)
                out_ref[pl.ds(first, rows), :] = mine_ref[at, lanes]
                out_ref[pl.ds(second, rows), :] = other_ref[at, lanes]

    outs = [((2 * mine.shape[0], used), mine.dtype)] * 2
    return local_call(kernel, outs, rank.reshape(1).astype(jnp.int32), mine, other)


def rows_backward(part_ref, unit_ref, inv_ref, gain_ref):
    total = part_ref[0].astype(WIDE)
    for i in range(1, part_ref.shape[0]):
        total = total + part_ref[i].astype(WIDE)
    unit = unit_ref[...]
    return total, unit, norm_backward(total, unit, inv_ref[...], gain_ref[...])


def middle_rows(parts, unit, inv_scale, gain, cotangent):
    sources, span, width = parts.shape

    def kernel(_, part_ref, unit_ref, inv_ref, gain_ref, cot_ref, grad_ref, low_ref, sum_ref):
        total, unit_rows, delta = rows_backward(part_ref, unit_ref, inv_ref, gain_ref)
        grad = cot_ref[...].astype(WIDE) + delta
        grad_ref[...] = grad
        low = grad.astype(LOW)
        for i in range(sources):
            low_ref[i] = low
        sum_ref[...] = jnp.zeros_like(sum_ref)
        sum_ref[0:1, :] = jnp.sum(total * unit_rows, axis=0, keepdims=True)
        sum_ref[1:2, :] = jnp.sum(total, axis=0, keepdims=True)
        sum_ref[2:3, :] = jnp.sum(grad, axis=0, keepdims=True)

    outs = [((span, width), WIDE), ((sources, span, width), LOW), ((8, width), WIDE)]
    return local_call(
        kernel, outs, jnp.zeros((1,), jnp.int32), parts, unit, inv_scale, gain, cotangent
    )


def final_rows(parts, unit, inv_scale, gain, grad, sums, hidden, outputs, joint):
    sources, span, width = parts.shape
    feats = width // sources
    count = 5
    extra = hidden.shape[0]
    small = -(-3 * (count + extra) // 16) * 16
    half, trio = joint.shape[1:]

    def kernel(
        _, part_ref, unit_ref, inv_ref, gain_ref, grad_ref, sum_ref, hidden_ref, out_rows_ref,
        joint_ref, out_ref, all_ref, wide_ref
    ):
        total, unit_rows, delta = rows_backward(part_ref, unit_ref, inv_ref, gain_ref)
        low = (grad_ref[...] + delta).astype(LOW)
        out_rows = out_rows_ref[...]
        all_ref[...] = sum_ref[...]
        all_ref[3:4, :] = jnp.sum(total * unit_rows, axis=0, keepdims=True)
        all_ref[4:5, :] = jnp.sum(total, axis=0, keepdims=True)
        for j in range(sources):
            lanes = slice(j * feats, (j + 1) * feats)
            out_ref[j, :span, :] = out_rows[:, lanes]
            out_ref[j, span : 2 * span, :] = low[:, lanes]
            wide_ref[...] = jnp.zeros_like(wide_ref)
            start = 0
            for value in (all_ref[:count, lanes], hidden_ref[...]):
                size = value.shape[0]
                high = value.astype(LOW).astype(WIDE)
                middle = (value - high).astype(LOW).astype(WIDE)
                for piece in (high, middle, value - high - middle):
                    wide_ref[start : start + size, :] = piece
                    start += size
            out_ref[j, 2 * span : 2 * span + small, :] = wide_ref[...].astype(LOW)
            out_ref[j, 2 * span + small :, :trio] = joint_ref[j]
            out_ref[j, 2 * span + small :, trio:] = jnp.zeros((half, feats - trio), LOW)

    outs = [((sources, 2 * span + small + half, feats), LOW)]
    arrays = (parts, unit, inv_scale, gain, grad, sums, hidden, outputs, joint)
    scratch = (pltpu.VMEM((8, width), WIDE), pltpu.VMEM((small, feats), WIDE))
    packed = local_call(kernel, outs, jnp.zeros((1,), jnp.int32), *arrays, scratch=scratch)[0]
    return packed, 2 * span + small


def make_body(n_dp, n_row, n_col):
    masks = []
    while (1 << len(masks)) < n_col:
        masks.append(1 << len(masks))
    paired = n_dp == 2

    def col_swap(value, mask):
        return lax.ppermute(value, "col", [(i, i ^ mask) for i in range(n_col)])

    def dp_swap(value):
        return lax.ppermute(value, "dp", [(0, 1), (1, 0)])

    def row_exchange(blocks):
        return lax.all_to_all(blocks, "row", 0, 0, tiled=True)

    def row_gather(value):
        return row_exchange(jnp.broadcast_to(value[None], (n_row,) + value.shape))

    def col_parts(value):
        parts = [value]
        for mask in reversed(masks):
            parts = parts + [col_swap(part, mask) for part in parts]
        return parts

    def align_lanes(part, offset, near):
        size = part.shape[1] // n_col
        source = [near.index(mine ^ offset) for mine in near]
        return jnp.concatenate([part[:, i * size : (i + 1) * size] for i in source], axis=1)

    def col_gather(value):
        return jnp.concatenate(col_parts(value), axis=0)

    def body(
        inputs,
        pre_gain,
        pre_shift,
        joint_weight,
        joint_bias,
        merge_weight,
        merge_bias,
        mid_gain,
        mid_shift,
        expand_weight,
        expand_bias,
        reduce_weight,
        reduce_bias,
        cotangent,
    ):
        row = lax.axis_index("row")
        col = lax.axis_index("col")
        rank = lax.axis_index("dp")
        near = [0]
        for mask in reversed(masks):
            near = near + [offset ^ mask for offset in near]
        tokens, feats = inputs.shape
        width = feats * n_row
        images = tokens // SEQ
        head_size = joint_bias.shape[2] // 2
        span = -(-tokens // (n_row * n_col * 16)) * 16
        padded = span * n_row * n_col
        block = span * n_row
        units = expand_weight.shape[1] // n_row
        trio = joint_weight.shape[1] // n_row

        def pad_rows(value):
            return jnp.pad(value, ((0, padded - value.shape[0]), (0, 0)))

        def join(value, other, bit, axis):
            low = jnp.where(bit == 0, value, other)
            high = jnp.where(bit == 0, other, value)
            return straight(jnp.concatenate([low, high], axis=axis))

        def half_of(value, index, axis):
            size = value.shape[axis] // 2
            return lax.dynamic_slice_in_dim(value, index * size, size, axis)

        def own_rows(value):
            return lax.dynamic_slice_in_dim(value, row * span, span, 0)

        def own_block(value):
            return lax.dynamic_slice_in_dim(pad_rows(value), col * block, block, 0)

        def everywhere(value):
            return [value] * n_row

        def fit_lanes(blocks):
            return [jnp.pad(b, ((0, 0), (0, feats - b.shape[1]))) for b in blocks]

        def pack(*pieces):
            return straight(jnp.stack([jnp.concatenate(group, axis=0) for group in zip(*pieces)]))

        def height(piece):
            return piece[0].shape[0]

        def lanes(blocks):
            return jnp.concatenate([blocks[i] for i in range(n_row)], axis=-1)

        def weight_move(value, parts):
            mine = half_of(value, rank, 0) if paired else value
            return [mine[:, j * parts : (j + 1) * parts] for j in range(n_row)]

        def weight_move_rows(value, parts):
            mine = half_of(value, rank, 1) if paired else value
            return [mine[j * parts : (j + 1) * parts].T for j in range(n_row)]

        def dp_rows(moved, groups):
            return join_halves(moved, dp_swap(moved), rank, groups) if paired else moved

        def grad_start(blocks):
            low = blocks.astype(LOW)
            if paired:
                sent = half_of(low, 1 - rank, 1)
                kept = half_of(low, rank, 1)
                low = (kept.astype(WIDE) + dp_swap(sent).astype(WIDE)).astype(LOW)
            elif n_dp > 1:
                low = lax.psum(blocks.astype(WIDE), "dp").astype(LOW)
            return low

        def grad_join(moved):
            return join(moved, dp_swap(moved), rank, 1) if paired else moved

        def sum_start(product, rows):
            size = padded // 2
            got = col_swap(product(rows[size:]).astype(LOW), masks[0])
            total = product(rows[:size]) + got.astype(WIDE)
            for mask in masks[1:]:
                size //= 2
                total = total[:size] + col_swap(total[size:].astype(LOW), mask).astype(WIDE)
            return total.astype(LOW).reshape(n_row, span, width)

        vectors = (pre_gain, pre_shift, merge_bias, mid_gain, mid_shift, reduce_bias)
        small = -(-3 * len(vectors) // 16) * 16
        first_out = pack_first(
            inputs, joint_weight, vectors, col, rank, block, padded, trio, 2 if paired else 1
        )
        first = row_exchange(first_out)
        cot_in, merge_in, expand_in, reduce_in = lax.optimization_barrier(
            (cotangent, merge_weight, expand_weight, reduce_weight, first_out)
        )[:4]
        second_out = pack(
            everywhere(own_block(cot_in)),
            everywhere(half_of(merge_in, rank, 0) if paired else merge_in),
        )
        third_out = pack(
            fit_lanes(weight_move(expand_in, units)), fit_lanes(weight_move_rows(reduce_in, units))
        )
        second = row_exchange(after(second_out, first))
        third = row_exchange(after(third_out, second))
        inner = block + small
        half = feats // 2 if paired else feats
        x_rows, small_full, joint_own = split_blocks(
            first,
            (
                (0, block, feats, True),
                (block, small, feats, True),
                (inner, half, trio, False),
            ),
        )
        small_full = merge_wide(small_full[:18])
        gain1, shift1, bias1, gain2, shift2, bias2 = [small_full[i : i + 1] for i in range(6)]
        x_full = col_gather(x_rows)
        joint_own = dp_rows(joint_own, n_row)
        cot_rows, merge_rows = split_blocks(
            second, ((0, block, feats, True), (block, half, feats, True))
        )
        mlp_part = mlp_blocks(third, half, units)

        residual = x_full.astype(WIDE)
        unit1, inv1 = norm_forward(residual)
        normed1 = (unit1 * gain1 + shift1).astype(LOW)
        own_bias = joint_bias.reshape(2 * head_size)
        bias_row = jnp.concatenate(
            [own_bias[:head_size], jnp.zeros((head_size,), WIDE), own_bias[head_size:]]
        )
        joint_rows = (dot(normed1, joint_own, 1, 0) + bias_row).astype(LOW)
        query_rows = joint_rows[:, :head_size]
        key_rows = joint_rows[:, head_size : 2 * head_size]
        value_rows = joint_rows[:, 2 * head_size :]
        order = jnp.concatenate([(col ^ offset) * block + jnp.arange(block) for offset in near])
        real = (order < tokens).astype(WIDE)
        factor = real[:, None] * head_size ** (-0.5)
        keep = real[None]
        if images > 1:
            keep = keep * (order[:, None] // SEQ == order[None] // SEQ).astype(WIDE)
        own_context, totals = attend(query_rows, key_rows, value_rows, factor, keep)

        merge_other = dp_swap(merge_rows) if paired else merge_rows
        merge_own = join_halves(merge_rows, merge_other, rank, 1) if paired else merge_rows
        merge_full = col_gather(merge_own)
        cot_full = col_gather(cot_rows)
        mlp_other = dp_swap(mlp_part) if paired else mlp_part

        group_context = row_gather(after(own_context, third, merge_other)).reshape(n_row * head_size, padded)
        expand_own, reduce_own = mlp_join(
            mlp_part, after(mlp_other, group_context), rank, n_row, units, paired
        )
        context_full = jnp.concatenate(
            [
                align_lanes(part, offset, near) if offset else part
                for part, offset in zip(col_parts(group_context), near)
            ],
            axis=0,
        )
        mixed1 = residual + dot(context_full, merge_full, 0, 0) + bias1
        unit2, inv2 = norm_forward(mixed1)
        normed2 = (unit2 * gain2 + shift2).astype(LOW)

        own_units = lax.dynamic_slice_in_dim(expand_bias, row * units, units, 0)
        hidden_pre = dot(normed2, expand_own, 1, 0) + own_units
        value, slope = gelu_pair(hidden_pre)
        active = value.astype(LOW)
        hidden_grad = (dot(cot_full, reduce_own, 1, 0) * slope).astype(LOW)
        normed2_total = sum_start(lambda rows: dot(rows, expand_own, 1, 1), hidden_grad)
        out_total = sum_start(
            lambda rows: dot(rows, reduce_own, 1, 1), after(active, normed2_total)
        )

        mixed_grad, mixed_low, sums = middle_rows(
            row_exchange(normed2_total),
            own_rows(unit2),
            own_rows(inv2),
            gain2,
            own_rows(cot_full),
        )
        mixed_block = row_exchange(mixed_low).reshape(block, width)
        mixed_low = col_gather(mixed_block)
        out_parts = row_exchange(after(out_total, mixed_block))
        out_rows = jnp.sum(out_parts.astype(WIDE), axis=0)
        out_rows = (own_rows(mixed1) + out_rows + bias2).astype(LOW)

        expand_grad = dot(normed2, hidden_grad, 0, 0).reshape(n_row, feats, units)
        reduce_grad = dot(cot_full, active, 0, 0).reshape(n_row, feats, units)
        mlp_grad = grad_start(
            jnp.concatenate([expand_grad.astype(LOW), reduce_grad.astype(LOW)], axis=2)
        )
        head_rows = lax.dynamic_slice_in_dim(merge_own, row * head_size, head_size, 0)
        context_grad = dot(mixed_low, head_rows, 1, 1).astype(LOW)
        mlp_moved = row_exchange(after(mlp_grad, context_grad, out_parts))
        mlp_grad = grad_join(mlp_moved)
        expand_weight_grad = (
            lanes(mlp_grad[..., :units]).astype(WIDE)
        )
        reduce_weight_grad = (
            jnp.concatenate([mlp_grad[j, :, units:].T for j in range(n_row)]).astype(WIDE)
        )

        query_grad, key_grad, value_grad = attend_back(
            query_rows, key_rows, value_rows, own_context, totals, context_grad, factor, keep
        )
        joint_grad = jnp.concatenate([query_grad, key_grad, value_grad], axis=-1).astype(LOW)
        joint_bias_grad = jnp.concatenate(
            [jnp.sum(query_grad, axis=0), jnp.sum(value_grad, axis=0)]
        )
        normed1_parts = row_exchange(sum_start(lambda rows: dot(rows, joint_own, 1, 1), joint_grad))

        joint_blocks = grad_start(dot(normed1, joint_grad, 0, 0).reshape(n_row, feats, trio))
        own_mixed = lax.dynamic_slice_in_dim(mixed_low, row * feats, feats, 1)
        merge_weight_grad = dot(group_context, own_mixed, 1, 0)
        if paired:
            merge_grad_low = merge_weight_grad.astype(LOW)
            merge_weight_grad = merge_grad_low.astype(WIDE) + dp_swap(merge_grad_low).astype(WIDE)
        elif n_dp > 1:
            merge_weight_grad = lax.psum(merge_weight_grad, "dp")

        hidden_sum = jnp.pad(
            jnp.sum(hidden_grad, axis=0, dtype=WIDE), (0, -units % feats)
        ).reshape(-1, feats)
        packed, ends = final_rows(
            normed1_parts,
            own_rows(unit1),
            own_rows(inv1),
            gain1,
            mixed_grad,
            sums,
            hidden_sum,
            out_rows,
            joint_blocks,
        )
        final = row_exchange(packed)
        vectors = final[:, 2 * span : ends]
        joint_blocks = grad_join(final[:, ends:, :trio])
        joint_weight_grad = lanes(joint_blocks).astype(WIDE)
        partial = jnp.sum(merge_wide(vectors[:, :15]), axis=0)
        hidden_all = merge_wide(vectors[:, 15 : 15 + 3 * hidden_sum.shape[0]]).reshape(n_row, -1)[:, :units].reshape(-1)
        local = jnp.concatenate([hidden_all, joint_bias_grad])
        local = jnp.pad(local, (0, -local.shape[0] % feats)).reshape(-1, feats)
        local = jnp.concatenate(
            [partial, jnp.sum(cotangent.astype(WIDE), axis=0)[None], local], axis=0
        )
        shared = lax.all_gather(
            jnp.concatenate(
                [final[:, : 2 * span].reshape(2 * block, feats), split_wide(local)], axis=0
            ),
            "col",
        )
        spread = shared[:, : 2 * block].reshape(n_col, n_row, 2 * span, feats)
        outputs = spread[:, :, :span].reshape(padded, feats)[:tokens]
        inputs_grad = spread[:, :, span:].reshape(padded, feats)[:tokens].astype(WIDE)
        shared = merge_wide(shared[:, 2 * block :])
        vector_sums = jnp.concatenate([jnp.sum(shared[:, :5], axis=0), pick(shared, col)[5:]])
        if paired:
            vector_sums = vector_sums + dp_swap(vector_sums)
        elif n_dp > 1:
            vector_sums = lax.psum(vector_sums, "dp")
        reduce_bias_grad = vector_sums[5]
        own_sums = vector_sums[6:].reshape(-1)
        mid_gain_grad, mid_shift_grad, merge_bias_grad, pre_gain_grad, pre_shift_grad = [
            vector_sums[i] for i in range(5)
        ]
        tail = n_row * units
        expand_bias_grad = own_sums[:tail]
        joint_bias_grad = own_sums[tail : tail + 2 * head_size].reshape(joint_bias.shape)
        return (
            outputs,
            inputs_grad,
            pre_gain_grad,
            pre_shift_grad,
            joint_weight_grad,
            joint_bias_grad,
            merge_weight_grad,
            merge_bias_grad,
            mid_gain_grad,
            mid_shift_grad,
            expand_weight_grad,
            expand_bias_grad,
            reduce_weight_grad,
            reduce_bias_grad,
        )

    return body


def solution(mesh):
    in_specs = (
        P("dp", "row"),
        P("row"),
        P("row"),
        P("row", "col"),
        P("col", "row", None),
        P("col", "row"),
        P("row"),
        P("row"),
        P("row"),
        P("row", "col"),
        P("col"),
        P("col", "row"),
        P("row"),
        P("dp", "row"),
    )
    out_specs = (
        P("dp", "row"),
        P("dp", "row"),
        P("row"),
        P("row"),
        P("row", "col"),
        P("col", "row", None),
        P("col", "row"),
        P("row"),
        P("row"),
        P("row"),
        P("row", "col"),
        P("col"),
        P("col", "row"),
        P("row"),
    )
    body = make_body(mesh.shape["dp"], mesh.shape["row"], mesh.shape["col"])
    return jax.shard_map(body, mesh=mesh, in_specs=in_specs, out_specs=out_specs, check_vma=False)
```

```python
import jax
import jax.numpy as jnp
from jax import lax
from jax.experimental import pallas as pl
from jax.experimental.layout import Layout, with_layout_constraint
from jax.experimental.pallas import tpu as pltpu
from jax.sharding import PartitionSpec as P

SEQ = 729


NORM_EPSILON = 1e-06
TANH_SLOPE = 0.7978845608028654
CUBIC_TERM = 0.044715
LOW = jnp.bfloat16
WIDE = jnp.float32


def gelu_pair(preact):
    inner_tanh = jnp.tanh(TANH_SLOPE * (preact + CUBIC_TERM * preact * preact * preact))
    value = 0.5 * preact * (1.0 + inner_tanh)
    slope = 0.5 * (1.0 + inner_tanh) + 0.5 * preact * (
        1.0 - inner_tanh * inner_tanh
    ) * TANH_SLOPE * (1.0 + 3.0 * CUBIC_TERM * preact * preact)
    return value, slope


def dot(left, right, left_dim, right_dim):
    return lax.dot_general(
        left, right, (((left_dim,), (right_dim,)), ((), ())), preferred_element_type=WIDE
    )


def pick(blocks, index, axis=0):
    return lax.dynamic_index_in_dim(blocks, index, axis, keepdims=False)


def after(values, *others):
    return lax.optimization_barrier((values,) + others)[0]


def straight(values):
    return with_layout_constraint(values, Layout(tuple(range(values.ndim))))


def norm_forward(values):
    row_mean = jnp.mean(values, axis=-1, keepdims=True)
    row_var = jnp.mean(values * values, axis=-1, keepdims=True) - row_mean * row_mean
    inv_scale = lax.rsqrt(row_var + NORM_EPSILON)
    return (values - row_mean) * inv_scale, inv_scale


def norm_backward(upstream, unit_rows, inv_scale, norm_gain):
    scaled = upstream * norm_gain
    first = jnp.mean(scaled, axis=-1, keepdims=True)
    second = jnp.mean(scaled * unit_rows, axis=-1, keepdims=True)
    return inv_scale * (scaled - first - unit_rows * second)


def attend(query_rows, key_rows, value_rows, factor, keep):
    scores = dot(query_rows, key_rows, 1, 1) * factor
    totals = jnp.log(jnp.sum(jnp.exp(scores) * keep, axis=-1, keepdims=True))
    softmax_rows = (jnp.exp(scores - totals) * keep).astype(LOW)
    return dot(value_rows, softmax_rows, 0, 1).astype(LOW), totals


def attend_back(query_rows, key_rows, value_rows, context, totals, upstream, factor, keep):
    scores = dot(query_rows, key_rows, 1, 1) * factor
    weights = jnp.exp(scores - totals) * keep
    value_grad = dot(weights.astype(LOW), upstream, 0, 0)
    prob_grad = dot(upstream, value_rows, 1, 1)
    row_delta = jnp.sum(
        upstream.astype(WIDE) * context.T.astype(WIDE), axis=-1, keepdims=True
    )
    score_grad = (weights * (prob_grad - row_delta)).astype(LOW)
    scale = query_rows.shape[-1] ** (-0.5)
    query_grad = dot(score_grad, key_rows, 1, 0) * scale
    key_grad = dot(score_grad, query_rows, 0, 0) * scale
    return query_grad, key_grad, value_grad


def split_wide(value):
    high = lax.reduce_precision(value, 8, 7)
    rest = value - high
    middle = lax.reduce_precision(rest, 8, 7)
    return jnp.concatenate([high, middle, rest - middle], axis=0).astype(LOW)


def merge_wide(rows):
    high, middle, last = jnp.split(rows.astype(WIDE), 3, axis=-2)
    return high + (middle + last)


def local_call(kernel, outs, scalars, *arrays, scratch=()):
    return pl.pallas_call(
        kernel,
        out_shape=[jax.ShapeDtypeStruct(shape, kind) for shape, kind in outs],
        grid_spec=pltpu.PrefetchScalarGridSpec(
            num_scalar_prefetch=1,
            grid=(1,),
            in_specs=[
                pl.BlockSpec(a.shape, lambda i, _, n=a.ndim: (0,) * n) for a in arrays
            ],
            out_specs=[
                pl.BlockSpec(shape, lambda i, _, n=len(shape): (0,) * n) for shape, _ in outs
            ],
            scratch_shapes=list(scratch),
        ),
    )(scalars, *arrays)


def split_blocks(moved, plan):
    sources = moved.shape[0]
    outs = []
    for _, rows, used, side in plan:
        shape = (rows, sources * used) if side else (sources * rows, used)
        outs.append((shape, moved.dtype))

    def kernel(_, moved_ref, *out_refs):
        for (start, rows, used, side), out_ref in zip(plan, out_refs):
            for i in range(sources):
                piece = moved_ref[i, start : start + rows, :used]
                if side:
                    out_ref[:, i * used : (i + 1) * used] = piece
                else:
                    out_ref[i * rows : (i + 1) * rows, :] = piece

    return local_call(kernel, outs, jnp.zeros((1,), jnp.int32), moved)


def pack_first(inputs, joint_weight, vectors, col, rank, block, padded, parts, halves):
    tokens, feats = inputs.shape
    count = len(vectors)
    small = -(-3 * count // 16) * 16
    half = feats // halves
    rows = block + small + half

    def kernel(place_ref, input_ref, joint_ref, *refs):
        vector_refs, (out_ref, wide_ref, token_ref) = refs[:count], refs[count:]
        token_ref[...] = jnp.zeros_like(token_ref)
        token_ref[:tokens, :] = input_ref[...]
        wide_ref[...] = jnp.zeros_like(wide_ref)
        for i, vector_ref in enumerate(vector_refs):
            value = vector_ref[...].reshape(1, feats)
            high = value.astype(LOW).astype(WIDE)
            middle = (value - high).astype(LOW).astype(WIDE)
            wide_ref[i : i + 1, :] = high
            wide_ref[count + i : count + i + 1, :] = middle
            wide_ref[2 * count + i : 2 * count + i + 1, :] = value - high - middle
        start = pl.multiple_of(place_ref[0] * block, 16)
        mine = token_ref[pl.ds(start, block), :]
        low = wide_ref[...].astype(LOW)
        joint = joint_ref[pl.ds(pl.multiple_of(place_ref[1] * half, 16), half), :]
        for j in range(out_ref.shape[0]):
            out_ref[j, :block, :] = mine
            out_ref[j, block : block + small, :] = low
            out_ref[j, block + small :, :parts] = joint[:, j * parts : (j + 1) * parts]
            out_ref[j, block + small :, parts:] = jnp.zeros((half, feats - parts), LOW)

    count_out = joint_weight.shape[1] // parts
    place_at = jnp.stack([col, rank if halves == 2 else 0 * rank]).astype(jnp.int32)
    return local_call(
        kernel,
        [((count_out, rows, feats), LOW)],
        place_at,
        inputs,
        joint_weight,
        *vectors,
        scratch=(pltpu.VMEM((small, feats), WIDE), pltpu.VMEM((padded, feats), LOW)),
    )[0]


def join_halves(mine, other, rank, groups):
    rows = mine.shape[0] // groups
    outs = [((2 * mine.shape[0], mine.shape[1]), mine.dtype)]

    def kernel(rank_ref, mine_ref, other_ref, out_ref):
        for i in range(groups):
            first = pl.multiple_of((2 * i + rank_ref[0]) * rows, 16)
            second = pl.multiple_of((2 * i + 1 - rank_ref[0]) * rows, 16)
            out_ref[pl.ds(first, rows), :] = mine_ref[i * rows : (i + 1) * rows, :]
            out_ref[pl.ds(second, rows), :] = other_ref[i * rows : (i + 1) * rows, :]

    return local_call(kernel, outs, rank.reshape(1).astype(jnp.int32), mine, other)[0]


def mlp_blocks(moved, rows, used):
    sources = moved.shape[0]

    def kernel(_, moved_ref, out_ref):
        for i in range(sources):
            at = slice(i * rows, (i + 1) * rows)
            out_ref[at, :used] = moved_ref[i, :rows, :used]
            out_ref[at, used : 2 * used] = moved_ref[i, rows:, :used]
            out_ref[at, 2 * used :] = jnp.zeros((rows, out_ref.shape[1] - 2 * used), LOW)

    outs = [((sources * rows, -(-2 * used // 128) * 128), moved.dtype)]
    return local_call(kernel, outs, jnp.zeros((1,), jnp.int32), moved)[0]


def mlp_join(mine, other, rank, groups, used, paired):
    if not paired:
        return mine[:, :used], mine[:, used : 2 * used]
    rows = mine.shape[0] // groups

    def kernel(rank_ref, mine_ref, other_ref, *out_refs):
        for i in range(groups):
            at = slice(i * rows, (i + 1) * rows)
            first = pl.multiple_of((2 * i + rank_ref[0]) * rows, 16)
            second = pl.multiple_of((2 * i + 1 - rank_ref[0]) * rows, 16)
            for k, out_ref in enumerate(out_refs):
                lanes = slice(k * used, (k + 1) * used)
                out_ref[pl.ds(first, rows), :] = mine_ref[at, lanes]
                out_ref[pl.ds(second, rows), :] = other_ref[at, lanes]

    outs = [((2 * mine.shape[0], used), mine.dtype)] * 2
    return local_call(kernel, outs, rank.reshape(1).astype(jnp.int32), mine, other)


def rows_backward(part_ref, unit_ref, inv_ref, gain_ref):
    total = part_ref[0].astype(WIDE)
    for i in range(1, part_ref.shape[0]):
        total = total + part_ref[i].astype(WIDE)
    unit = unit_ref[...]
    return total, unit, norm_backward(total, unit, inv_ref[...], gain_ref[...])


def middle_rows(parts, unit, inv_scale, gain, cotangent):
    sources, span, width = parts.shape

    def kernel(_, part_ref, unit_ref, inv_ref, gain_ref, cot_ref, grad_ref, low_ref, sum_ref):
        total, unit_rows, delta = rows_backward(part_ref, unit_ref, inv_ref, gain_ref)
        grad = cot_ref[...].astype(WIDE) + delta
        grad_ref[...] = grad
        low = grad.astype(LOW)
        for i in range(sources):
            low_ref[i] = low
        sum_ref[...] = jnp.zeros_like(sum_ref)
        sum_ref[0:1, :] = jnp.sum(total * unit_rows, axis=0, keepdims=True)
        sum_ref[1:2, :] = jnp.sum(total, axis=0, keepdims=True)
        sum_ref[2:3, :] = jnp.sum(grad, axis=0, keepdims=True)

    outs = [((span, width), WIDE), ((sources, span, width), LOW), ((8, width), WIDE)]
    return local_call(
        kernel, outs, jnp.zeros((1,), jnp.int32), parts, unit, inv_scale, gain, cotangent
    )


def final_rows(parts, unit, inv_scale, gain, grad, sums, hidden, outputs, joint):
    sources, span, width = parts.shape
    feats = width // sources
    count = 5
    extra = hidden.shape[0]
    small = -(-3 * (count + extra) // 16) * 16
    half, trio = joint.shape[1:]

    def kernel(
        _, part_ref, unit_ref, inv_ref, gain_ref, grad_ref, sum_ref, hidden_ref, out_rows_ref,
        joint_ref, out_ref, all_ref, wide_ref
    ):
        total, unit_rows, delta = rows_backward(part_ref, unit_ref, inv_ref, gain_ref)
        low = (grad_ref[...] + delta).astype(LOW)
        out_rows = out_rows_ref[...]
        all_ref[...] = sum_ref[...]
        all_ref[3:4, :] = jnp.sum(total * unit_rows, axis=0, keepdims=True)
        all_ref[4:5, :] = jnp.sum(total, axis=0, keepdims=True)
        for j in range(sources):
            lanes = slice(j * feats, (j + 1) * feats)
            out_ref[j, :span, :] = out_rows[:, lanes]
            out_ref[j, span : 2 * span, :] = low[:, lanes]
            wide_ref[...] = jnp.zeros_like(wide_ref)
            start = 0
            for value in (all_ref[:count, lanes], hidden_ref[...]):
                size = value.shape[0]
                high = value.astype(LOW).astype(WIDE)
                middle = (value - high).astype(LOW).astype(WIDE)
                for piece in (high, middle, value - high - middle):
                    wide_ref[start : start + size, :] = piece
                    start += size
            out_ref[j, 2 * span : 2 * span + small, :] = wide_ref[...].astype(LOW)
            out_ref[j, 2 * span + small :, :trio] = joint_ref[j]
            out_ref[j, 2 * span + small :, trio:] = jnp.zeros((half, feats - trio), LOW)

    outs = [((sources, 2 * span + small + half, feats), LOW)]
    arrays = (parts, unit, inv_scale, gain, grad, sums, hidden, outputs, joint)
    scratch = (pltpu.VMEM((8, width), WIDE), pltpu.VMEM((small, feats), WIDE))
    packed = local_call(kernel, outs, jnp.zeros((1,), jnp.int32), *arrays, scratch=scratch)[0]
    return packed, 2 * span + small


def make_body(n_dp, n_row, n_col):
    masks = []
    while (1 << len(masks)) < n_col:
        masks.append(1 << len(masks))
    paired = n_dp == 2

    def col_swap(value, mask):
        return lax.ppermute(value, "col", [(i, i ^ mask) for i in range(n_col)])

    def dp_swap(value):
        return lax.ppermute(value, "dp", [(0, 1), (1, 0)])

    def row_exchange(blocks):
        return lax.all_to_all(blocks, "row", 0, 0, tiled=True)

    def row_gather(value):
        return row_exchange(jnp.broadcast_to(value[None], (n_row,) + value.shape))

    def col_parts(value):
        parts = [value]
        for mask in reversed(masks):
            parts = parts + [col_swap(part, mask) for part in parts]
        return parts

    def align_lanes(part, offset, near):
        size = part.shape[1] // n_col
        source = [near.index(mine ^ offset) for mine in near]
        return jnp.concatenate([part[:, i * size : (i + 1) * size] for i in source], axis=1)

    def col_gather(value):
        return jnp.concatenate(col_parts(value), axis=0)

    def body(
        inputs,
        pre_gain,
        pre_shift,
        joint_weight,
        joint_bias,
        merge_weight,
        merge_bias,
        mid_gain,
        mid_shift,
        expand_weight,
        expand_bias,
        reduce_weight,
        reduce_bias,
        cotangent,
    ):
        row = lax.axis_index("row")
        col = lax.axis_index("col")
        rank = lax.axis_index("dp")
        near = [0]
        for mask in reversed(masks):
            near = near + [offset ^ mask for offset in near]
        tokens, feats = inputs.shape
        width = feats * n_row
        images = tokens // SEQ
        head_size = joint_bias.shape[2] // 2
        span = -(-tokens // (n_row * n_col * 16)) * 16
        padded = span * n_row * n_col
        block = span * n_row
        units = expand_weight.shape[1] // n_row
        trio = joint_weight.shape[1] // n_row

        def pad_rows(value):
            return jnp.pad(value, ((0, padded - value.shape[0]), (0, 0)))

        def join(value, other, bit, axis):
            low = jnp.where(bit == 0, value, other)
            high = jnp.where(bit == 0, other, value)
            return straight(jnp.concatenate([low, high], axis=axis))

        def half_of(value, index, axis):
            size = value.shape[axis] // 2
            return lax.dynamic_slice_in_dim(value, index * size, size, axis)

        def own_rows(value):
            return lax.dynamic_slice_in_dim(value, row * span, span, 0)

        def own_block(value):
            return lax.dynamic_slice_in_dim(pad_rows(value), col * block, block, 0)

        def everywhere(value):
            return [value] * n_row

        def fit_lanes(blocks):
            return [jnp.pad(b, ((0, 0), (0, feats - b.shape[1]))) for b in blocks]

        def pack(*pieces):
            return straight(jnp.stack([jnp.concatenate(group, axis=0) for group in zip(*pieces)]))

        def lanes(blocks):
            return jnp.concatenate([blocks[i] for i in range(n_row)], axis=-1)

        def weight_move(value, parts):
            mine = half_of(value, rank, 0) if paired else value
            return [mine[:, j * parts : (j + 1) * parts] for j in range(n_row)]

        def weight_move_rows(value, parts):
            mine = half_of(value, rank, 1) if paired else value
            return [mine[j * parts : (j + 1) * parts].T for j in range(n_row)]

        def dp_rows(moved, groups):
            return join_halves(moved, dp_swap(moved), rank, groups) if paired else moved

        def grad_start(blocks):
            low = blocks.astype(LOW)
            if paired:
                sent = half_of(low, 1 - rank, 1)
                kept = half_of(low, rank, 1)
                low = (kept.astype(WIDE) + dp_swap(sent).astype(WIDE)).astype(LOW)
            elif n_dp > 1:
                low = lax.psum(blocks.astype(WIDE), "dp").astype(LOW)
            return low

        def grad_join(moved):
            return join(moved, dp_swap(moved), rank, 1) if paired else moved

        def sum_start(product, rows):
            size = padded // 2
            sent = product(rows[size:]).astype(LOW)
            got = col_swap(sent, masks[0])
            total = product(rows[:size]) + got.astype(WIDE)
            for mask in masks[1:]:
                size //= 2
                got = col_swap(total[size:].astype(LOW), mask)
                total = total[:size] + got.astype(WIDE)
            return total.astype(LOW).reshape(n_row, span, width)

        vectors = (pre_gain, pre_shift, merge_bias, mid_gain, mid_shift, reduce_bias)
        small = -(-3 * len(vectors) // 16) * 16
        first_out = pack_first(
            inputs, joint_weight, vectors, col, rank, block, padded, trio, 2 if paired else 1
        )
        first = row_exchange(first_out)
        cot_in, merge_in, expand_in, reduce_in = lax.optimization_barrier(
            (cotangent, merge_weight, expand_weight, reduce_weight, first_out)
        )[:4]
        second_out = pack(
            everywhere(own_block(cot_in)),
            everywhere(half_of(merge_in, rank, 0) if paired else merge_in),
        )
        third_out = pack(
            fit_lanes(weight_move(expand_in, units)), fit_lanes(weight_move_rows(reduce_in, units))
        )
        second = row_exchange(after(second_out, first))
        third = row_exchange(after(third_out, second))
        inner = block + small
        half = feats // 2 if paired else feats
        x_rows, small_full, joint_own = split_blocks(
            first,
            (
                (0, block, feats, True),
                (block, small, feats, True),
                (inner, half, trio, False),
            ),
        )
        small_full = merge_wide(small_full[:18])
        gain1, shift1, bias1, gain2, shift2, bias2 = [small_full[i : i + 1] for i in range(6)]
        x_full = col_gather(x_rows)
        joint_own = dp_rows(joint_own, n_row)
        cot_rows, merge_rows = split_blocks(
            second, ((0, block, feats, True), (block, half, feats, True))
        )
        mlp_part = mlp_blocks(third, half, units)

        residual = x_full.astype(WIDE)
        unit1, inv1 = norm_forward(residual)
        normed1 = (unit1 * gain1 + shift1).astype(LOW)
        own_bias = joint_bias.reshape(2 * head_size)
        bias_row = jnp.concatenate(
            [own_bias[:head_size], jnp.zeros((head_size,), WIDE), own_bias[head_size:]]
        )
        joint_rows = (dot(normed1, joint_own, 1, 0) + bias_row).astype(LOW)
        query_rows = joint_rows[:, :head_size]
        key_rows = joint_rows[:, head_size : 2 * head_size]
        value_rows = joint_rows[:, 2 * head_size :]
        order = jnp.concatenate([(col ^ offset) * block + jnp.arange(block) for offset in near])
        real = (order < tokens).astype(WIDE)
        factor = real[:, None] * head_size ** (-0.5)
        keep = real[None]
        if images > 1:
            keep = keep * (order[:, None] // SEQ == order[None] // SEQ).astype(WIDE)
        own_context, totals = attend(query_rows, key_rows, value_rows, factor, keep)

        merge_other = dp_swap(merge_rows) if paired else merge_rows
        merge_own = join_halves(merge_rows, merge_other, rank, 1) if paired else merge_rows
        merge_full = col_gather(merge_own)
        cot_full = col_gather(cot_rows)
        mlp_other = dp_swap(mlp_part) if paired else mlp_part

        group_context = row_gather(after(own_context, third, merge_other)).reshape(n_row * head_size, padded)
        context_parts = col_parts(group_context)
        expand_own, reduce_own = mlp_join(
            mlp_part, after(mlp_other, context_parts[-1]), rank, n_row, units, paired
        )
        context_full = jnp.concatenate(
            [
                align_lanes(part, offset, near) if offset else part
                for part, offset in zip(context_parts, near)
            ],
            axis=0,
        )
        mixed1 = residual + dot(context_full, merge_full, 0, 0) + bias1
        unit2, inv2 = norm_forward(mixed1)
        normed2 = (unit2 * gain2 + shift2).astype(LOW)

        own_units = lax.dynamic_slice_in_dim(expand_bias, row * units, units, 0)
        hidden_pre = dot(normed2, expand_own, 1, 0) + own_units
        value, slope = gelu_pair(hidden_pre)
        active = value.astype(LOW)
        hidden_grad = (dot(cot_full, reduce_own, 1, 0) * slope).astype(LOW)
        normed2_total = sum_start(lambda rows: dot(rows, expand_own, 1, 1), hidden_grad)
        out_total = sum_start(
            lambda rows: dot(rows, reduce_own, 1, 1), after(active, normed2_total)
        )

        unit2_own, inv2_own, cot_own = own_rows(unit2), own_rows(inv2), own_rows(cot_full)
        normed2_parts = row_exchange(normed2_total)

        mixed_grad, mixed_low, sums = middle_rows(
            normed2_parts,
            unit2_own,
            inv2_own,
            gain2,
            cot_own,
        )
        mixed_block = row_exchange(mixed_low).reshape(block, width)
        mixed_low = col_gather(mixed_block)
        out_parts = row_exchange(after(out_total, mixed_block))
        out_rows = jnp.sum(out_parts.astype(WIDE), axis=0)
        out_rows = (own_rows(mixed1) + out_rows + bias2).astype(LOW)

        expand_grad = dot(normed2, hidden_grad, 0, 0).astype(LOW)
        reduce_grad = dot(cot_full, active, 0, 0).astype(LOW)
        expand_grad = expand_grad.reshape(n_row, feats, units)
        reduce_grad = reduce_grad.reshape(n_row, feats, units)
        mlp_grad = grad_start(jnp.concatenate([expand_grad, reduce_grad], axis=2))
        head_rows = lax.dynamic_slice_in_dim(merge_own, row * head_size, head_size, 0)
        context_grad = dot(mixed_low, head_rows, 1, 1).astype(LOW)
        mlp_moved = row_exchange(after(mlp_grad, out_parts))
        mlp_grad = grad_join(mlp_moved)
        expand_weight_grad = (
            lanes(mlp_grad[..., :units]).astype(WIDE)
        )
        reduce_weight_grad = (
            jnp.concatenate([mlp_grad[j, :, units:].T for j in range(n_row)]).astype(WIDE)
        )

        query_grad, key_grad, value_grad = attend_back(
            query_rows, key_rows, value_rows, own_context, totals, context_grad, factor, keep
        )
        joint_grad = jnp.concatenate([query_grad, key_grad, value_grad], axis=-1).astype(LOW)
        joint_bias_grad = jnp.concatenate(
            [jnp.sum(query_grad, axis=0), jnp.sum(value_grad, axis=0)]
        )
        normed1_parts = row_exchange(sum_start(lambda rows: dot(rows, joint_own, 1, 1), joint_grad))

        joint_blocks = grad_start(dot(normed1, joint_grad, 0, 0).reshape(n_row, feats, trio))
        own_mixed = lax.dynamic_slice_in_dim(mixed_low, row * feats, feats, 1)
        merge_weight_grad = dot(group_context, own_mixed, 1, 0)
        if paired:
            merge_grad_low = merge_weight_grad.astype(LOW)
            merge_weight_grad = merge_grad_low.astype(WIDE) + dp_swap(merge_grad_low).astype(WIDE)
        elif n_dp > 1:
            merge_weight_grad = lax.psum(merge_weight_grad, "dp")

        hidden_sum = jnp.pad(
            jnp.sum(hidden_grad, axis=0, dtype=WIDE), (0, -units % feats)
        ).reshape(-1, feats)
        packed, ends = final_rows(
            normed1_parts,
            own_rows(unit1),
            own_rows(inv1),
            gain1,
            mixed_grad,
            sums,
            hidden_sum,
            out_rows,
            joint_blocks,
        )
        final = row_exchange(packed)
        vectors = final[:, 2 * span : ends]
        joint_blocks = grad_join(final[:, ends:, :trio])
        joint_weight_grad = lanes(joint_blocks).astype(WIDE)
        partial = jnp.sum(merge_wide(vectors[:, :15]), axis=0)
        hidden_all = merge_wide(vectors[:, 15 : 15 + 3 * hidden_sum.shape[0]]).reshape(n_row, -1)[:, :units].reshape(-1)
        local = jnp.concatenate([hidden_all, joint_bias_grad])
        local = jnp.pad(local, (0, -local.shape[0] % feats)).reshape(-1, feats)
        local = jnp.concatenate(
            [partial, jnp.sum(cotangent.astype(WIDE), axis=0)[None], local], axis=0
        )
        spread_in = jnp.concatenate(
            [final[:, : 2 * span].reshape(2 * block, feats), split_wide(local)], axis=0
        )
        shared = lax.all_gather(spread_in, "col")
        spread = shared[:, : 2 * block].reshape(n_col, n_row, 2 * span, feats)
        outputs = spread[:, :, :span].reshape(padded, feats)[:tokens]
        inputs_grad = spread[:, :, span:].reshape(padded, feats)[:tokens].astype(WIDE)
        shared = merge_wide(shared[:, 2 * block :])
        vector_sums = jnp.concatenate([jnp.sum(shared[:, :5], axis=0), pick(shared, col)[5:]])
        if paired:
            vector_sums = vector_sums + dp_swap(vector_sums)
        elif n_dp > 1:
            vector_sums = lax.psum(vector_sums, "dp")
        reduce_bias_grad = vector_sums[5]
        own_sums = vector_sums[6:].reshape(-1)
        mid_gain_grad, mid_shift_grad, merge_bias_grad, pre_gain_grad, pre_shift_grad = [
            vector_sums[i] for i in range(5)
        ]
        tail = n_row * units
        expand_bias_grad = own_sums[:tail]
        joint_bias_grad = own_sums[tail : tail + 2 * head_size].reshape(joint_bias.shape)
        return (
            outputs,
            inputs_grad,
            pre_gain_grad,
            pre_shift_grad,
            joint_weight_grad,
            joint_bias_grad,
            merge_weight_grad,
            merge_bias_grad,
            mid_gain_grad,
            mid_shift_grad,
            expand_weight_grad,
            expand_bias_grad,
            reduce_weight_grad,
            reduce_bias_grad,
        )

    return body


def solution(mesh):
    in_specs = (
        P("dp", "row"),
        P("row"),
        P("row"),
        P("row", "col"),
        P("col", "row", None),
        P("col", "row"),
        P("row"),
        P("row"),
        P("row"),
        P("row", "col"),
        P("col"),
        P("col", "row"),
        P("row"),
        P("dp", "row"),
    )
    out_specs = (
        P("dp", "row"),
        P("dp", "row"),
        P("row"),
        P("row"),
        P("row", "col"),
        P("col", "row", None),
        P("col", "row"),
        P("row"),
        P("row"),
        P("row"),
        P("row", "col"),
        P("col"),
        P("col", "row"),
        P("row"),
    )
    body = make_body(mesh.shape["dp"], mesh.shape["row"], mesh.shape["col"])

    return jax.shard_map(body, mesh=mesh, in_specs=in_specs, out_specs=out_specs, check_vma=False)
```

```python
import jax
import jax.numpy as jnp
from jax import lax
from jax.experimental import pallas as pl
from jax.experimental.layout import Layout, with_layout_constraint
from jax.experimental.pallas import tpu as pltpu
from jax.sharding import PartitionSpec as P

SEQ = 729


NORM_EPSILON = 1e-06
TANH_SLOPE = 0.7978845608028654
CUBIC_TERM = 0.044715
LOW = jnp.bfloat16
WIDE = jnp.float32


def gelu_pair(preact):
    inner_tanh = jnp.tanh(TANH_SLOPE * (preact + CUBIC_TERM * preact * preact * preact))
    value = 0.5 * preact * (1.0 + inner_tanh)
    slope = 0.5 * (1.0 + inner_tanh) + 0.5 * preact * (
        1.0 - inner_tanh * inner_tanh
    ) * TANH_SLOPE * (1.0 + 3.0 * CUBIC_TERM * preact * preact)
    return value, slope


def dot(left, right, left_dim, right_dim):
    return lax.dot_general(
        left, right, (((left_dim,), (right_dim,)), ((), ())), preferred_element_type=WIDE
    )


def pick(blocks, index, axis=0):
    return lax.dynamic_index_in_dim(blocks, index, axis, keepdims=False)


def after(values, *others):
    return lax.optimization_barrier((values,) + others)[0]


def straight(values):
    return with_layout_constraint(values, Layout(tuple(range(values.ndim))))


def norm_forward(values):
    row_mean = jnp.mean(values, axis=-1, keepdims=True)
    row_var = jnp.mean(values * values, axis=-1, keepdims=True) - row_mean * row_mean
    inv_scale = lax.rsqrt(row_var + NORM_EPSILON)
    return (values - row_mean) * inv_scale, inv_scale


def norm_backward(upstream, unit_rows, inv_scale, norm_gain):
    scaled = upstream * norm_gain
    first = jnp.mean(scaled, axis=-1, keepdims=True)
    second = jnp.mean(scaled * unit_rows, axis=-1, keepdims=True)
    return inv_scale * (scaled - first - unit_rows * second)


def attend(query_rows, key_rows, value_rows, factor, keep):
    scores = dot(query_rows, key_rows, 1, 1) * factor
    totals = jnp.log(jnp.sum(jnp.exp(scores) * keep, axis=-1, keepdims=True))
    softmax_rows = (jnp.exp(scores - totals) * keep).astype(LOW)
    return dot(value_rows, softmax_rows, 0, 1).astype(LOW), totals


def attend_back(query_rows, key_rows, value_rows, context, totals, upstream, factor, keep):
    scores = dot(query_rows, key_rows, 1, 1) * factor
    weights = jnp.exp(scores - totals) * keep
    value_grad = dot(weights.astype(LOW), upstream, 0, 0)
    prob_grad = dot(upstream, value_rows, 1, 1)
    row_delta = jnp.sum(
        upstream.astype(WIDE) * context.T.astype(WIDE), axis=-1, keepdims=True
    )
    score_grad = (weights * (prob_grad - row_delta)).astype(LOW)
    scale = query_rows.shape[-1] ** (-0.5)
    query_grad = dot(score_grad, key_rows, 1, 0) * scale
    key_grad = dot(score_grad, query_rows, 0, 0) * scale
    return query_grad, key_grad, value_grad


def split_wide(value):
    high = lax.reduce_precision(value, 8, 7)
    rest = value - high
    middle = lax.reduce_precision(rest, 8, 7)
    return jnp.concatenate([high, middle, rest - middle], axis=0).astype(LOW)


def merge_wide(rows):
    high, middle, last = jnp.split(rows.astype(WIDE), 3, axis=-2)
    return high + (middle + last)


def local_call(kernel, outs, scalars, *arrays, scratch=()):
    return pl.pallas_call(
        kernel,
        out_shape=[jax.ShapeDtypeStruct(shape, kind) for shape, kind in outs],
        grid_spec=pltpu.PrefetchScalarGridSpec(
            num_scalar_prefetch=1,
            grid=(1,),
            in_specs=[
                pl.BlockSpec(a.shape, lambda i, _, n=a.ndim: (0,) * n) for a in arrays
            ],
            out_specs=[
                pl.BlockSpec(shape, lambda i, _, n=len(shape): (0,) * n) for shape, _ in outs
            ],
            scratch_shapes=list(scratch),
        ),
    )(scalars, *arrays)


def split_blocks(moved, plan):
    sources = moved.shape[0]
    outs = []
    for _, rows, used, side in plan:
        shape = (rows, sources * used) if side else (sources * rows, used)
        outs.append((shape, moved.dtype))

    def kernel(_, moved_ref, *out_refs):
        for (start, rows, used, side), out_ref in zip(plan, out_refs):
            for i in range(sources):
                piece = moved_ref[i, start : start + rows, :used]
                if side:
                    out_ref[:, i * used : (i + 1) * used] = piece
                else:
                    out_ref[i * rows : (i + 1) * rows, :] = piece

    return local_call(kernel, outs, jnp.zeros((1,), jnp.int32), moved)


def pack_first(inputs, joint_weight, vectors, col, rank, block, padded, parts, halves):
    tokens, feats = inputs.shape
    count = len(vectors)
    small = -(-3 * count // 16) * 16
    half = feats // halves
    rows = block + small + half

    def kernel(place_ref, input_ref, joint_ref, *refs):
        vector_refs, (out_ref, wide_ref, token_ref) = refs[:count], refs[count:]
        token_ref[...] = jnp.zeros_like(token_ref)
        token_ref[:tokens, :] = input_ref[...]
        wide_ref[...] = jnp.zeros_like(wide_ref)
        for i, vector_ref in enumerate(vector_refs):
            value = vector_ref[...].reshape(1, feats)
            high = value.astype(LOW).astype(WIDE)
            middle = (value - high).astype(LOW).astype(WIDE)
            wide_ref[i : i + 1, :] = high
            wide_ref[count + i : count + i + 1, :] = middle
            wide_ref[2 * count + i : 2 * count + i + 1, :] = value - high - middle
        start = pl.multiple_of(place_ref[0] * block, 16)
        mine = token_ref[pl.ds(start, block), :]
        low = wide_ref[...].astype(LOW)
        joint = joint_ref[pl.ds(pl.multiple_of(place_ref[1] * half, 16), half), :]
        for j in range(out_ref.shape[0]):
            out_ref[j, :block, :] = mine
            out_ref[j, block : block + small, :] = low
            out_ref[j, block + small :, :parts] = joint[:, j * parts : (j + 1) * parts]
            out_ref[j, block + small :, parts:] = jnp.zeros((half, feats - parts), LOW)

    count_out = joint_weight.shape[1] // parts
    place_at = jnp.stack([col, rank if halves == 2 else 0 * rank]).astype(jnp.int32)
    return local_call(
        kernel,
        [((count_out, rows, feats), LOW)],
        place_at,
        inputs,
        joint_weight,
        *vectors,
        scratch=(pltpu.VMEM((small, feats), WIDE), pltpu.VMEM((padded, feats), LOW)),
    )[0]


def join_halves(mine, other, rank, groups):
    rows = mine.shape[0] // groups
    outs = [((2 * mine.shape[0], mine.shape[1]), mine.dtype)]

    def kernel(rank_ref, mine_ref, other_ref, out_ref):
        for i in range(groups):
            first = pl.multiple_of((2 * i + rank_ref[0]) * rows, 16)
            second = pl.multiple_of((2 * i + 1 - rank_ref[0]) * rows, 16)
            out_ref[pl.ds(first, rows), :] = mine_ref[i * rows : (i + 1) * rows, :]
            out_ref[pl.ds(second, rows), :] = other_ref[i * rows : (i + 1) * rows, :]

    return local_call(kernel, outs, rank.reshape(1).astype(jnp.int32), mine, other)[0]


def mlp_join(mine, other, rank, groups, used, paired):
    if not paired:
        return mine[:, :used], mine[:, used : 2 * used]
    rows = mine.shape[0] // groups

    def kernel(rank_ref, mine_ref, other_ref, *out_refs):
        for i in range(groups):
            at = slice(i * rows, (i + 1) * rows)
            first = pl.multiple_of((2 * i + rank_ref[0]) * rows, 16)
            second = pl.multiple_of((2 * i + 1 - rank_ref[0]) * rows, 16)
            for k, out_ref in enumerate(out_refs):
                lanes = slice(k * used, (k + 1) * used)
                out_ref[pl.ds(first, rows), :] = mine_ref[at, lanes]
                out_ref[pl.ds(second, rows), :] = other_ref[at, lanes]

    outs = [((2 * mine.shape[0], used), mine.dtype)] * 2
    return local_call(kernel, outs, rank.reshape(1).astype(jnp.int32), mine, other)


def rows_backward(part_ref, unit_ref, inv_ref, gain_ref):
    total = part_ref[0].astype(WIDE)
    for i in range(1, part_ref.shape[0]):
        total = total + part_ref[i].astype(WIDE)
    unit = unit_ref[...]
    return total, unit, norm_backward(total, unit, inv_ref[...], gain_ref[...])


def middle_rows(parts, unit, inv_scale, gain, cotangent):
    sources, span, width = parts.shape

    def kernel(_, part_ref, unit_ref, inv_ref, gain_ref, cot_ref, grad_ref, low_ref, sum_ref):
        total, unit_rows, delta = rows_backward(part_ref, unit_ref, inv_ref, gain_ref)
        grad = cot_ref[...].astype(WIDE) + delta
        grad_ref[...] = grad
        low = grad.astype(LOW)
        for i in range(sources):
            low_ref[i] = low
        sum_ref[...] = jnp.zeros_like(sum_ref)
        sum_ref[0:1, :] = jnp.sum(total * unit_rows, axis=0, keepdims=True)
        sum_ref[1:2, :] = jnp.sum(total, axis=0, keepdims=True)
        sum_ref[2:3, :] = jnp.sum(grad, axis=0, keepdims=True)

    outs = [((span, width), WIDE), ((sources, span, width), LOW), ((8, width), WIDE)]
    return local_call(
        kernel, outs, jnp.zeros((1,), jnp.int32), parts, unit, inv_scale, gain, cotangent
    )


def final_rows(parts, unit, inv_scale, gain, grad, sums, hidden, outputs, joint):
    sources, span, width = parts.shape
    feats = width // sources
    count = 5
    extra = hidden.shape[0]
    small = -(-3 * (count + extra) // 16) * 16
    half, trio = joint.shape[1:]

    def kernel(
        _, part_ref, unit_ref, inv_ref, gain_ref, grad_ref, sum_ref, hidden_ref, out_rows_ref,
        joint_ref, out_ref, all_ref, wide_ref
    ):
        total, unit_rows, delta = rows_backward(part_ref, unit_ref, inv_ref, gain_ref)
        low = (grad_ref[...] + delta).astype(LOW)
        out_rows = out_rows_ref[...]
        all_ref[...] = sum_ref[...]
        all_ref[3:4, :] = jnp.sum(total * unit_rows, axis=0, keepdims=True)
        all_ref[4:5, :] = jnp.sum(total, axis=0, keepdims=True)
        for j in range(sources):
            lanes = slice(j * feats, (j + 1) * feats)
            out_ref[j, :span, :] = out_rows[:, lanes]
            out_ref[j, span : 2 * span, :] = low[:, lanes]
            wide_ref[...] = jnp.zeros_like(wide_ref)
            start = 0
            for value in (all_ref[:count, lanes], hidden_ref[...]):
                size = value.shape[0]
                high = value.astype(LOW).astype(WIDE)
                middle = (value - high).astype(LOW).astype(WIDE)
                for piece in (high, middle, value - high - middle):
                    wide_ref[start : start + size, :] = piece
                    start += size
            out_ref[j, 2 * span : 2 * span + small, :] = wide_ref[...].astype(LOW)
            out_ref[j, 2 * span + small :, :trio] = joint_ref[j]
            out_ref[j, 2 * span + small :, trio:] = jnp.zeros((half, feats - trio), LOW)

    outs = [((sources, 2 * span + small + half, feats), LOW)]
    arrays = (parts, unit, inv_scale, gain, grad, sums, hidden, outputs, joint)
    scratch = (pltpu.VMEM((8, width), WIDE), pltpu.VMEM((small, feats), WIDE))
    packed = local_call(kernel, outs, jnp.zeros((1,), jnp.int32), *arrays, scratch=scratch)[0]
    return packed, 2 * span + small


def make_body(n_dp, n_row, n_col):
    masks = []
    while (1 << len(masks)) < n_col:
        masks.append(1 << len(masks))
    paired = n_dp == 2

    def col_swap(value, mask):
        return lax.ppermute(value, "col", [(i, i ^ mask) for i in range(n_col)])

    def dp_swap(value):
        return lax.ppermute(value, "dp", [(0, 1), (1, 0)])

    def row_exchange(blocks):
        return lax.all_to_all(blocks, "row", 0, 0, tiled=True)

    def row_gather(value):
        return row_exchange(jnp.broadcast_to(value[None], (n_row,) + value.shape))

    def col_parts(value):
        parts = [value]
        for mask in reversed(masks):
            parts = parts + [col_swap(part, mask) for part in parts]
        return parts

    def align_lanes(part, offset, near):
        size = part.shape[1] // n_col
        source = [near.index(mine ^ offset) for mine in near]
        return jnp.concatenate([part[:, i * size : (i + 1) * size] for i in source], axis=1)

    def col_gather(value):
        return jnp.concatenate(col_parts(value), axis=0)

    def body(
        inputs,
        pre_gain,
        pre_shift,
        joint_weight,
        joint_bias,
        merge_weight,
        merge_bias,
        mid_gain,
        mid_shift,
        expand_weight,
        expand_bias,
        reduce_weight,
        reduce_bias,
        cotangent,
    ):
        row = lax.axis_index("row")
        col = lax.axis_index("col")
        rank = lax.axis_index("dp")
        near = [0]
        for mask in reversed(masks):
            near = near + [offset ^ mask for offset in near]
        tokens, feats = inputs.shape
        width = feats * n_row
        images = tokens // SEQ
        head_size = joint_bias.shape[2] // 2
        span = -(-tokens // (n_row * n_col * 16)) * 16
        padded = span * n_row * n_col
        block = span * n_row
        units = expand_weight.shape[1] // n_row
        trio = joint_weight.shape[1] // n_row

        def pad_rows(value):
            return jnp.pad(value, ((0, padded - value.shape[0]), (0, 0)))

        def join(value, other, bit, axis):
            low = jnp.where(bit == 0, value, other)
            high = jnp.where(bit == 0, other, value)
            return straight(jnp.concatenate([low, high], axis=axis))

        def half_of(value, index, axis):
            size = value.shape[axis] // 2
            return lax.dynamic_slice_in_dim(value, index * size, size, axis)

        def own_rows(value):
            return lax.dynamic_slice_in_dim(value, row * span, span, 0)

        def own_block(value):
            return lax.dynamic_slice_in_dim(pad_rows(value), col * block, block, 0)

        def everywhere(value):
            return [value] * n_row

        def pack(*pieces):
            return straight(jnp.stack([jnp.concatenate(group, axis=0) for group in zip(*pieces)]))

        def lanes(blocks):
            return jnp.concatenate([blocks[i] for i in range(n_row)], axis=-1)

        def weight_move(value, parts):
            mine = half_of(value, rank, 0) if paired else value
            return [mine[:, j * parts : (j + 1) * parts] for j in range(n_row)]

        def weight_move_rows(value, parts):
            mine = half_of(value, rank, 1) if paired else value
            return [mine[j * parts : (j + 1) * parts].T for j in range(n_row)]

        def dp_rows(moved, groups):
            return join_halves(moved, dp_swap(moved), rank, groups) if paired else moved

        def grad_start(blocks):
            low = blocks.astype(LOW)
            if paired:
                sent = half_of(low, 1 - rank, 1)
                kept = half_of(low, rank, 1)
                low = (kept.astype(WIDE) + dp_swap(sent).astype(WIDE)).astype(LOW)
            elif n_dp > 1:
                low = lax.psum(blocks.astype(WIDE), "dp").astype(LOW)
            return low

        def grad_join(moved):
            return join(moved, dp_swap(moved), rank, 1) if paired else moved

        def sum_start(product, rows):
            size = padded // 2
            sent = product(rows[size:]).astype(LOW)
            got = col_swap(sent, masks[0])
            total = product(rows[:size]) + got.astype(WIDE)
            for mask in masks[1:]:
                size //= 2
                got = col_swap(total[size:].astype(LOW), mask)
                total = total[:size] + got.astype(WIDE)
            return total.astype(LOW).reshape(n_row, span, width)

        vectors = (pre_gain, pre_shift, merge_bias, mid_gain, mid_shift, reduce_bias)
        small = -(-3 * len(vectors) // 16) * 16
        first_out = pack_first(
            inputs, joint_weight, vectors, col, rank, block, padded, trio, 2 if paired else 1
        )
        first = row_exchange(first_out)
        cot_in, merge_in, expand_in, reduce_in = lax.optimization_barrier(
            (cotangent, merge_weight, expand_weight, reduce_weight, first_out)
        )[:4]
        second_out = pack(
            everywhere(own_block(cot_in)),
            everywhere(half_of(merge_in, rank, 0) if paired else merge_in),
        )
        mlp_lanes = -(-2 * units // 128) * 128
        third_out = straight(
            jnp.stack(
                [
                    jnp.pad(
                        jnp.concatenate([e, r], axis=1), ((0, 0), (0, mlp_lanes - 2 * units))
                    )
                    for e, r in zip(
                        weight_move(expand_in, units), weight_move_rows(reduce_in, units)
                    )
                ]
            )
        )
        second = row_exchange(after(second_out, first))
        third = row_exchange(after(third_out, second))
        inner = block + small
        half = feats // 2 if paired else feats
        x_rows, small_full, joint_own = split_blocks(
            first,
            (
                (0, block, feats, True),
                (block, small, feats, True),
                (inner, half, trio, False),
            ),
        )
        small_full = merge_wide(small_full[:18])
        gain1, shift1, bias1, gain2, shift2, bias2 = [small_full[i : i + 1] for i in range(6)]
        x_full = col_gather(x_rows)
        joint_own = dp_rows(joint_own, n_row)
        cot_rows, merge_rows = split_blocks(
            second, ((0, block, feats, True), (block, half, feats, True))
        )
        mlp_part = third.reshape(n_row * half, mlp_lanes)

        residual = x_full.astype(WIDE)
        unit1, inv1 = norm_forward(residual)
        normed1 = (unit1 * gain1 + shift1).astype(LOW)
        own_bias = joint_bias.reshape(2 * head_size)
        bias_row = jnp.concatenate(
            [own_bias[:head_size], jnp.zeros((head_size,), WIDE), own_bias[head_size:]]
        )
        joint_rows = (dot(normed1, joint_own, 1, 0) + bias_row).astype(LOW)
        query_rows = joint_rows[:, :head_size]
        key_rows = joint_rows[:, head_size : 2 * head_size]
        value_rows = joint_rows[:, 2 * head_size :]
        order = jnp.concatenate([(col ^ offset) * block + jnp.arange(block) for offset in near])
        real = (order < tokens).astype(WIDE)
        factor = real[:, None] * head_size ** (-0.5)
        keep = real[None]
        if images > 1:
            keep = keep * (order[:, None] // SEQ == order[None] // SEQ).astype(WIDE)
        own_context, totals = attend(query_rows, key_rows, value_rows, factor, keep)

        merge_other = dp_swap(merge_rows) if paired else merge_rows
        merge_own = join_halves(merge_rows, merge_other, rank, 1) if paired else merge_rows
        merge_full = col_gather(merge_own)
        cot_full = col_gather(cot_rows)
        mlp_other = dp_swap(mlp_part) if paired else mlp_part

        group_context = row_gather(after(own_context, third, merge_other)).reshape(n_row * head_size, padded)
        context_parts = col_parts(group_context)
        mlp_other = after(mlp_other, group_context)
        expand_own, reduce_own = mlp_join(mlp_part, mlp_other, rank, n_row, units, paired)
        context_full = jnp.concatenate(
            [
                align_lanes(part, offset, near) if offset else part
                for part, offset in zip(context_parts, near)
            ],
            axis=0,
        )
        mixed1 = residual + dot(context_full, merge_full, 0, 0) + bias1
        unit2, inv2 = norm_forward(mixed1)
        normed2 = (unit2 * gain2 + shift2).astype(LOW)

        own_units = lax.dynamic_slice_in_dim(expand_bias, row * units, units, 0)
        hidden_pre = dot(normed2, expand_own, 1, 0) + own_units
        value, slope = gelu_pair(hidden_pre)
        active = value.astype(LOW)
        hidden_grad = (dot(cot_full, reduce_own, 1, 0) * slope).astype(LOW)
        normed2_total = sum_start(lambda rows: dot(rows, expand_own, 1, 1), hidden_grad)
        out_total = sum_start(
            lambda rows: dot(rows, reduce_own, 1, 1), after(active, normed2_total)
        )

        unit2_own, inv2_own, cot_own = own_rows(unit2), own_rows(inv2), own_rows(cot_full)
        normed2_parts = row_exchange(normed2_total)

        mixed_grad, mixed_low, sums = middle_rows(
            normed2_parts,
            unit2_own,
            inv2_own,
            gain2,
            cot_own,
        )
        mixed_block = row_exchange(mixed_low).reshape(block, width)
        mixed_low = col_gather(mixed_block)
        out_parts = row_exchange(after(out_total, mixed_block))
        out_rows = jnp.sum(out_parts.astype(WIDE), axis=0)
        out_rows = (own_rows(mixed1) + out_rows + bias2).astype(LOW)

        expand_grad = dot(normed2, hidden_grad, 0, 0).astype(LOW)
        reduce_grad = dot(cot_full, active, 0, 0).astype(LOW)
        expand_grad = expand_grad.reshape(n_row, feats, units)
        reduce_grad = reduce_grad.reshape(n_row, feats, units)
        mlp_grad = grad_start(jnp.concatenate([expand_grad, reduce_grad], axis=2))
        head_rows = lax.dynamic_slice_in_dim(merge_own, row * head_size, head_size, 0)
        context_grad = dot(mixed_low, head_rows, 1, 1).astype(LOW)
        mlp_moved = row_exchange(after(mlp_grad, out_parts))
        mlp_grad = grad_join(mlp_moved)
        expand_weight_grad = (
            lanes(mlp_grad[..., :units]).astype(WIDE)
        )
        reduce_weight_grad = (
            jnp.concatenate([mlp_grad[j, :, units:].T for j in range(n_row)]).astype(WIDE)
        )

        query_grad, key_grad, value_grad = attend_back(
            query_rows, key_rows, value_rows, own_context, totals, context_grad, factor, keep
        )
        joint_grad = jnp.concatenate([query_grad, key_grad, value_grad], axis=-1).astype(LOW)
        joint_bias_grad = jnp.concatenate(
            [jnp.sum(query_grad, axis=0), jnp.sum(value_grad, axis=0)]
        )
        normed1_parts = row_exchange(sum_start(lambda rows: dot(rows, joint_own, 1, 1), joint_grad))

        joint_blocks = grad_start(dot(normed1, joint_grad, 0, 0).reshape(n_row, feats, trio))
        own_mixed = lax.dynamic_slice_in_dim(mixed_low, row * feats, feats, 1)
        merge_weight_grad = dot(group_context, own_mixed, 1, 0)
        if paired:
            merge_grad_low = merge_weight_grad.astype(LOW)
            merge_weight_grad = merge_grad_low.astype(WIDE) + dp_swap(merge_grad_low).astype(WIDE)
        elif n_dp > 1:
            merge_weight_grad = lax.psum(merge_weight_grad, "dp")

        hidden_sum = jnp.pad(
            jnp.sum(hidden_grad, axis=0, dtype=WIDE), (0, -units % feats)
        ).reshape(-1, feats)
        packed, ends = final_rows(
            normed1_parts,
            own_rows(unit1),
            own_rows(inv1),
            gain1,
            mixed_grad,
            sums,
            hidden_sum,
            out_rows,
            joint_blocks,
        )
        final = row_exchange(packed)
        vectors = final[:, 2 * span : ends]
        joint_blocks = grad_join(final[:, ends:, :trio])
        joint_weight_grad = lanes(joint_blocks).astype(WIDE)
        partial = jnp.sum(merge_wide(vectors[:, :15]), axis=0)
        hidden_all = merge_wide(vectors[:, 15 : 15 + 3 * hidden_sum.shape[0]]).reshape(n_row, -1)[:, :units].reshape(-1)
        local = jnp.concatenate([hidden_all, joint_bias_grad])
        local = jnp.pad(local, (0, -local.shape[0] % feats)).reshape(-1, feats)
        local = jnp.concatenate(
            [partial, jnp.sum(cotangent.astype(WIDE), axis=0)[None], local], axis=0
        )
        spread_in = jnp.concatenate(
            [final[:, : 2 * span].reshape(2 * block, feats), split_wide(local)], axis=0
        )
        shared = lax.all_gather(spread_in, "col")
        spread = shared[:, : 2 * block].reshape(n_col, n_row, 2 * span, feats)
        outputs = spread[:, :, :span].reshape(padded, feats)[:tokens]
        inputs_grad = spread[:, :, span:].reshape(padded, feats)[:tokens].astype(WIDE)
        shared = merge_wide(shared[:, 2 * block :])
        vector_sums = jnp.concatenate([jnp.sum(shared[:, :5], axis=0), pick(shared, col)[5:]])
        if paired:
            vector_sums = vector_sums + dp_swap(vector_sums)
        elif n_dp > 1:
            vector_sums = lax.psum(vector_sums, "dp")
        reduce_bias_grad = vector_sums[5]
        own_sums = vector_sums[6:].reshape(-1)
        mid_gain_grad, mid_shift_grad, merge_bias_grad, pre_gain_grad, pre_shift_grad = [
            vector_sums[i] for i in range(5)
        ]
        tail = n_row * units
        expand_bias_grad = own_sums[:tail]
        joint_bias_grad = own_sums[tail : tail + 2 * head_size].reshape(joint_bias.shape)
        return (
            outputs,
            inputs_grad,
            pre_gain_grad,
            pre_shift_grad,
            joint_weight_grad,
            joint_bias_grad,
            merge_weight_grad,
            merge_bias_grad,
            mid_gain_grad,
            mid_shift_grad,
            expand_weight_grad,
            expand_bias_grad,
            reduce_weight_grad,
            reduce_bias_grad,
        )

    return body


def solution(mesh):
    in_specs = (
        P("dp", "row"),
        P("row"),
        P("row"),
        P("row", "col"),
        P("col", "row", None),
        P("col", "row"),
        P("row"),
        P("row"),
        P("row"),
        P("row", "col"),
        P("col"),
        P("col", "row"),
        P("row"),
        P("dp", "row"),
    )
    out_specs = (
        P("dp", "row"),
        P("dp", "row"),
        P("row"),
        P("row"),
        P("row", "col"),
        P("col", "row", None),
        P("col", "row"),
        P("row"),
        P("row"),
        P("row"),
        P("row", "col"),
        P("col"),
        P("col", "row"),
        P("row"),
    )
    body = make_body(mesh.shape["dp"], mesh.shape["row"], mesh.shape["col"])

    return jax.shard_map(body, mesh=mesh, in_specs=in_specs, out_specs=out_specs, check_vma=False)
```

```python
import jax
import jax.numpy as jnp
from jax import lax
from jax.experimental import pallas as pl
from jax.experimental.layout import Layout, with_layout_constraint
from jax.experimental.pallas import tpu as pltpu
from jax.sharding import PartitionSpec as P

SEQ = 729


NORM_EPSILON = 1e-06
TANH_SLOPE = 0.7978845608028654
CUBIC_TERM = 0.044715
LOW = jnp.bfloat16
WIDE = jnp.float32


def gelu_pair(preact):
    inner_tanh = jnp.tanh(TANH_SLOPE * (preact + CUBIC_TERM * preact * preact * preact))
    value = 0.5 * preact * (1.0 + inner_tanh)
    slope = 0.5 * (1.0 + inner_tanh) + 0.5 * preact * (
        1.0 - inner_tanh * inner_tanh
    ) * TANH_SLOPE * (1.0 + 3.0 * CUBIC_TERM * preact * preact)
    return value, slope


def dot(left, right, left_dim, right_dim):
    return lax.dot_general(
        left, right, (((left_dim,), (right_dim,)), ((), ())), preferred_element_type=WIDE
    )


def pick(blocks, index, axis=0):
    return lax.dynamic_index_in_dim(blocks, index, axis, keepdims=False)


def place(blocks, block, index):
    return lax.dynamic_update_index_in_dim(blocks, block, index, 0)


def after(values, *others):
    return lax.optimization_barrier((values,) + others)[0]


def straight(values):
    return with_layout_constraint(values, Layout(tuple(range(values.ndim))))


def norm_forward(values):
    row_mean = jnp.mean(values, axis=-1, keepdims=True)
    row_var = jnp.mean(values * values, axis=-1, keepdims=True) - row_mean * row_mean
    inv_scale = lax.rsqrt(row_var + NORM_EPSILON)
    return (values - row_mean) * inv_scale, inv_scale


def norm_backward(upstream, unit_rows, inv_scale, norm_gain):
    scaled = upstream * norm_gain
    first = jnp.mean(scaled, axis=-1, keepdims=True)
    second = jnp.mean(scaled * unit_rows, axis=-1, keepdims=True)
    return inv_scale * (scaled - first - unit_rows * second)


def attend(query_rows, key_rows, value_rows, factor, keep):
    scores = dot(query_rows, key_rows, 1, 1) * factor
    totals = jnp.log(jnp.sum(jnp.exp(scores) * keep, axis=-1, keepdims=True))
    softmax_rows = (jnp.exp(scores - totals) * keep).astype(LOW)
    return dot(value_rows, softmax_rows, 0, 1).astype(LOW), totals


def attend_back(query_rows, key_rows, value_rows, context, totals, upstream, factor, keep):
    scores = dot(query_rows, key_rows, 1, 1) * factor
    weights = jnp.exp(scores - totals) * keep
    value_grad = dot(weights.astype(LOW), upstream, 0, 0)
    prob_grad = dot(upstream, value_rows, 1, 1)
    row_delta = jnp.sum(
        upstream.astype(WIDE) * context.T.astype(WIDE), axis=-1, keepdims=True
    )
    score_grad = (weights * (prob_grad - row_delta)).astype(LOW)
    scale = query_rows.shape[-1] ** (-0.5)
    query_grad = dot(score_grad, key_rows, 1, 0) * scale
    key_grad = dot(score_grad, query_rows, 0, 0) * scale
    return query_grad, key_grad, value_grad


def split_wide(value):
    high = lax.reduce_precision(value, 8, 7)
    rest = value - high
    middle = lax.reduce_precision(rest, 8, 7)
    return jnp.concatenate([high, middle, rest - middle], axis=0).astype(LOW)


def merge_wide(rows):
    high, middle, last = jnp.split(rows.astype(WIDE), 3, axis=-2)
    return high + (middle + last)


def local_call(kernel, outs, scalars, *arrays, scratch=()):
    return pl.pallas_call(
        kernel,
        out_shape=[jax.ShapeDtypeStruct(shape, kind) for shape, kind in outs],
        grid_spec=pltpu.PrefetchScalarGridSpec(
            num_scalar_prefetch=1,
            grid=(1,),
            in_specs=[
                pl.BlockSpec(a.shape, lambda i, _, n=a.ndim: (0,) * n) for a in arrays
            ],
            out_specs=[
                pl.BlockSpec(shape, lambda i, _, n=len(shape): (0,) * n) for shape, _ in outs
            ],
            scratch_shapes=list(scratch),
        ),
    )(scalars, *arrays)


def split_blocks(moved, plan):
    sources = moved.shape[0]
    outs = []
    for _, rows, used, side in plan:
        shape = (rows, sources * used) if side else (sources * rows, used)
        outs.append((shape, moved.dtype))

    def kernel(_, moved_ref, *out_refs):
        for (start, rows, used, side), out_ref in zip(plan, out_refs):
            for i in range(sources):
                piece = moved_ref[i, start : start + rows, :used]
                if side:
                    out_ref[:, i * used : (i + 1) * used] = piece
                else:
                    out_ref[i * rows : (i + 1) * rows, :] = piece

    return local_call(kernel, outs, jnp.zeros((1,), jnp.int32), moved)


def pack_first(inputs, joint_weight, vectors, col, rank, block, padded, parts, halves):
    tokens, feats = inputs.shape
    count = len(vectors)
    small = -(-3 * count // 16) * 16
    half = feats // halves
    rows = block + small + half

    def kernel(place_ref, input_ref, joint_ref, *refs):
        vector_refs, (out_ref, wide_ref, token_ref) = refs[:count], refs[count:]
        token_ref[...] = jnp.zeros_like(token_ref)
        token_ref[:tokens, :] = input_ref[...]
        wide_ref[...] = jnp.zeros_like(wide_ref)
        for i, vector_ref in enumerate(vector_refs):
            value = vector_ref[...].reshape(1, feats)
            high = value.astype(LOW).astype(WIDE)
            middle = (value - high).astype(LOW).astype(WIDE)
            wide_ref[i : i + 1, :] = high
            wide_ref[count + i : count + i + 1, :] = middle
            wide_ref[2 * count + i : 2 * count + i + 1, :] = value - high - middle
        start = pl.multiple_of(place_ref[0] * block, 16)
        mine = token_ref[pl.ds(start, block), :]
        low = wide_ref[...].astype(LOW)
        joint = joint_ref[pl.ds(pl.multiple_of(place_ref[1] * half, 16), half), :]
        for j in range(out_ref.shape[0]):
            out_ref[j, :block, :] = mine
            out_ref[j, block : block + small, :] = low
            out_ref[j, block + small :, :parts] = joint[:, j * parts : (j + 1) * parts]
            out_ref[j, block + small :, parts:] = jnp.zeros((half, feats - parts), LOW)

    count_out = joint_weight.shape[1] // parts
    place_at = jnp.stack([col, rank if halves == 2 else 0 * rank]).astype(jnp.int32)
    return local_call(
        kernel,
        [((count_out, rows, feats), LOW)],
        place_at,
        inputs,
        joint_weight,
        *vectors,
        scratch=(pltpu.VMEM((small, feats), WIDE), pltpu.VMEM((padded, feats), LOW)),
    )[0]


def join_halves(mine, other, rank, groups):
    rows = mine.shape[0] // groups
    outs = [((2 * mine.shape[0], mine.shape[1]), mine.dtype)]

    def kernel(rank_ref, mine_ref, other_ref, out_ref):
        @pl.loop(0, groups)
        def _(i):
            at = pl.ds(pl.multiple_of(i * rows, 16), rows)
            first = pl.multiple_of((2 * i + rank_ref[0]) * rows, 16)
            second = pl.multiple_of((2 * i + 1 - rank_ref[0]) * rows, 16)
            out_ref[pl.ds(first, rows), :] = mine_ref[at, :]
            out_ref[pl.ds(second, rows), :] = other_ref[at, :]

    return local_call(kernel, outs, rank.reshape(1).astype(jnp.int32), mine, other)[0]


def mlp_join(mine, other, rank, groups, used, paired):
    if not paired:
        return mine[:, :used], mine[:, used : 2 * used]
    rows = mine.shape[0] // groups

    def kernel(rank_ref, mine_ref, other_ref, *out_refs):
        @pl.loop(0, groups)
        def _(i):
            at = pl.ds(pl.multiple_of(i * rows, 16), rows)
            first = pl.multiple_of((2 * i + rank_ref[0]) * rows, 16)
            second = pl.multiple_of((2 * i + 1 - rank_ref[0]) * rows, 16)
            for k, out_ref in enumerate(out_refs):
                lanes = slice(k * used, (k + 1) * used)
                out_ref[pl.ds(first, rows), :] = mine_ref[at, lanes]
                out_ref[pl.ds(second, rows), :] = other_ref[at, lanes]

    outs = [((2 * mine.shape[0], used), mine.dtype)] * 2
    return local_call(kernel, outs, rank.reshape(1).astype(jnp.int32), mine, other)


def rows_backward(part_ref, unit_ref, inv_ref, gain_ref):
    total = part_ref[0].astype(WIDE)
    for i in range(1, part_ref.shape[0]):
        total = total + part_ref[i].astype(WIDE)
    unit = unit_ref[...]
    return total, unit, norm_backward(total, unit, inv_ref[...], gain_ref[...])


def middle_rows(parts, unit, inv_scale, gain, cotangent):
    sources, span, width = parts.shape

    def kernel(_, part_ref, unit_ref, inv_ref, gain_ref, cot_ref, grad_ref, low_ref, sum_ref):
        total, unit_rows, delta = rows_backward(part_ref, unit_ref, inv_ref, gain_ref)
        grad = cot_ref[...].astype(WIDE) + delta
        grad_ref[...] = grad
        low = grad.astype(LOW)
        for i in range(sources):
            low_ref[i] = low
        sum_ref[...] = jnp.zeros_like(sum_ref)
        sum_ref[0:1, :] = jnp.sum(total * unit_rows, axis=0, keepdims=True)
        sum_ref[1:2, :] = jnp.sum(total, axis=0, keepdims=True)
        sum_ref[2:3, :] = jnp.sum(grad, axis=0, keepdims=True)

    outs = [((span, width), WIDE), ((sources, span, width), LOW), ((8, width), WIDE)]
    return local_call(
        kernel, outs, jnp.zeros((1,), jnp.int32), parts, unit, inv_scale, gain, cotangent
    )


def final_rows(parts, unit, inv_scale, gain, grad, sums, hidden, outputs, joint):
    sources, span, width = parts.shape
    feats = width // sources
    count = 5
    extra = hidden.shape[0]
    small = -(-3 * (count + extra) // 16) * 16
    half, trio = joint.shape[1:]

    def kernel(
        _, part_ref, unit_ref, inv_ref, gain_ref, grad_ref, sum_ref, hidden_ref, out_rows_ref,
        joint_ref, out_ref, all_ref, wide_ref
    ):
        total, unit_rows, delta = rows_backward(part_ref, unit_ref, inv_ref, gain_ref)
        low = (grad_ref[...] + delta).astype(LOW)
        out_rows = out_rows_ref[...]
        all_ref[...] = sum_ref[...]
        all_ref[3:4, :] = jnp.sum(total * unit_rows, axis=0, keepdims=True)
        all_ref[4:5, :] = jnp.sum(total, axis=0, keepdims=True)
        for j in range(sources):
            lanes = slice(j * feats, (j + 1) * feats)
            out_ref[j, :span, :] = out_rows[:, lanes]
            out_ref[j, span : 2 * span, :] = low[:, lanes]
            wide_ref[...] = jnp.zeros_like(wide_ref)
            start = 0
            for value in (all_ref[:count, lanes], hidden_ref[...]):
                size = value.shape[0]
                high = value.astype(LOW).astype(WIDE)
                middle = (value - high).astype(LOW).astype(WIDE)
                for piece in (high, middle, value - high - middle):
                    wide_ref[start : start + size, :] = piece
                    start += size
            out_ref[j, 2 * span : 2 * span + small, :] = wide_ref[...].astype(LOW)
            out_ref[j, 2 * span + small :, :trio] = joint_ref[j]
            out_ref[j, 2 * span + small :, trio:] = jnp.zeros((half, feats - trio), LOW)

    outs = [((sources, 2 * span + small + half, feats), LOW)]
    arrays = (parts, unit, inv_scale, gain, grad, sums, hidden, outputs, joint)
    scratch = (pltpu.VMEM((8, width), WIDE), pltpu.VMEM((small, feats), WIDE))
    packed = local_call(kernel, outs, jnp.zeros((1,), jnp.int32), *arrays, scratch=scratch)[0]
    return packed, 2 * span + small


def make_body(n_dp, n_row, n_col):
    masks = []
    while (1 << len(masks)) < n_col:
        masks.append(1 << len(masks))
    paired = n_dp == 2

    def col_swap(value, mask):
        return lax.ppermute(value, "col", [(i, i ^ mask) for i in range(n_col)])

    def dp_swap(value):
        return lax.ppermute(value, "dp", [(0, 1), (1, 0)])

    def row_exchange(blocks):
        return lax.all_to_all(blocks, "row", 0, 0, tiled=True)

    def row_share(value):
        row = lax.axis_index("row")
        blocks = jnp.zeros((n_row,) + value.shape, value.dtype)
        for k in range(n_row):
            pairs = [(i, (i + k) % n_row) for i in range(n_row)]
            piece = lax.ppermute(value, "row", pairs) if k else value
            blocks = place(blocks, piece, (row - k) % n_row)
        return blocks

    def col_parts(value):
        parts = [value]
        for mask in reversed(masks):
            parts = parts + [col_swap(part, mask) for part in parts]
        return parts

    def align_lanes(part, offset, near):
        size = part.shape[1] // n_col
        source = [near.index(mine ^ offset) for mine in near]
        return jnp.concatenate([part[:, i * size : (i + 1) * size] for i in source], axis=1)

    def col_gather(value):
        return jnp.concatenate(col_parts(value), axis=0)

    def body(
        inputs,
        pre_gain,
        pre_shift,
        joint_weight,
        joint_bias,
        merge_weight,
        merge_bias,
        mid_gain,
        mid_shift,
        expand_weight,
        expand_bias,
        reduce_weight,
        reduce_bias,
        cotangent,
    ):
        row = lax.axis_index("row")
        col = lax.axis_index("col")
        rank = lax.axis_index("dp")
        near = [0]
        for mask in reversed(masks):
            near = near + [offset ^ mask for offset in near]
        tokens, feats = inputs.shape
        width = feats * n_row
        images = tokens // SEQ
        head_size = joint_bias.shape[2] // 2
        span = -(-tokens // (n_row * n_col * 16)) * 16
        padded = span * n_row * n_col
        block = span * n_row
        units = expand_weight.shape[1] // n_row
        trio = joint_weight.shape[1] // n_row

        def pad_rows(value):
            return jnp.pad(value, ((0, padded - value.shape[0]), (0, 0)))

        def join(value, other, bit, axis):
            low = jnp.where(bit == 0, value, other)
            high = jnp.where(bit == 0, other, value)
            return straight(jnp.concatenate([low, high], axis=axis))

        def half_of(value, index, axis):
            size = value.shape[axis] // 2
            return lax.dynamic_slice_in_dim(value, index * size, size, axis)

        def own_rows(value):
            return lax.dynamic_slice_in_dim(value, row * span, span, 0)

        def own_block(value):
            return lax.dynamic_slice_in_dim(pad_rows(value), col * block, block, 0)

        def everywhere(value):
            return [value] * n_row

        def pack(*pieces):
            return straight(jnp.stack([jnp.concatenate(group, axis=0) for group in zip(*pieces)]))

        def lanes(blocks):
            return jnp.concatenate([blocks[i] for i in range(n_row)], axis=-1)

        def weight_move(value, parts):
            mine = half_of(value, rank, 0) if paired else value
            return [mine[:, j * parts : (j + 1) * parts] for j in range(n_row)]

        def weight_move_rows(value, parts):
            mine = half_of(value, rank, 1) if paired else value
            return [mine[j * parts : (j + 1) * parts].T for j in range(n_row)]

        def dp_rows(moved, groups):
            return join_halves(moved, dp_swap(moved), rank, groups) if paired else moved

        def grad_start(blocks):
            low = blocks.astype(LOW)
            if paired:
                sent = half_of(low, 1 - rank, 1)
                kept = half_of(low, rank, 1)
                low = (kept.astype(WIDE) + dp_swap(sent).astype(WIDE)).astype(LOW)
            elif n_dp > 1:
                low = lax.psum(blocks.astype(WIDE), "dp").astype(LOW)
            return low

        def grad_join(moved):
            return join(moved, dp_swap(moved), rank, 1) if paired else moved

        def sum_start(product, rows):
            size = padded // 2
            sent = product(rows[size:]).astype(LOW)
            got = col_swap(sent, masks[0])
            total = product(rows[:size]) + got.astype(WIDE)
            for mask in masks[1:]:
                size //= 2
                got = col_swap(total[size:].astype(LOW), mask)
                total = total[:size] + got.astype(WIDE)
            return total.astype(LOW).reshape(n_row, span, width)

        vectors = (pre_gain, pre_shift, merge_bias, mid_gain, mid_shift, reduce_bias)
        small = -(-3 * len(vectors) // 16) * 16
        first_out = pack_first(
            inputs, joint_weight, vectors, col, rank, block, padded, trio, 2 if paired else 1
        )
        first = row_exchange(first_out)
        cot_in, merge_in, expand_in, reduce_in = lax.optimization_barrier(
            (cotangent, merge_weight, expand_weight, reduce_weight, first_out)
        )[:4]
        second_out = pack(
            everywhere(own_block(cot_in)),
            everywhere(half_of(merge_in, rank, 0) if paired else merge_in),
        )
        mlp_lanes = -(-2 * units // 128) * 128
        third_out = straight(
            jnp.stack(
                [
                    jnp.pad(
                        jnp.concatenate([e, r], axis=1), ((0, 0), (0, mlp_lanes - 2 * units))
                    )
                    for e, r in zip(
                        weight_move(expand_in, units), weight_move_rows(reduce_in, units)
                    )
                ]
            )
        )
        second = row_exchange(after(second_out, first))
        third = row_exchange(after(third_out, second))
        inner = block + small
        half = feats // 2 if paired else feats
        x_rows, small_full, joint_own = split_blocks(
            first,
            (
                (0, block, feats, True),
                (block, small, feats, True),
                (inner, half, trio, False),
            ),
        )
        small_full = merge_wide(small_full[:18])
        gain1, shift1, bias1, gain2, shift2, bias2 = [small_full[i : i + 1] for i in range(6)]
        x_full = col_gather(x_rows)
        joint_own = dp_rows(joint_own, n_row)
        cot_rows, merge_rows = split_blocks(
            second, ((0, block, feats, True), (block, half, feats, True))
        )
        mlp_part = third.reshape(n_row * half, mlp_lanes)

        residual = x_full.astype(WIDE)
        unit1, inv1 = norm_forward(residual)
        normed1 = (unit1 * gain1 + shift1).astype(LOW)
        own_bias = joint_bias.reshape(2 * head_size)
        bias_row = jnp.concatenate(
            [own_bias[:head_size], jnp.zeros((head_size,), WIDE), own_bias[head_size:]]
        )
        joint_rows = (dot(normed1, joint_own, 1, 0) + bias_row).astype(LOW)
        query_rows = joint_rows[:, :head_size]
        key_rows = joint_rows[:, head_size : 2 * head_size]
        value_rows = joint_rows[:, 2 * head_size :]
        order = jnp.concatenate([(col ^ offset) * block + jnp.arange(block) for offset in near])
        real = (order < tokens).astype(WIDE)
        factor = real[:, None] * head_size ** (-0.5)
        keep = real[None]
        if images > 1:
            keep = keep * (order[:, None] // SEQ == order[None] // SEQ).astype(WIDE)
        own_context, totals = attend(query_rows, key_rows, value_rows, factor, keep)

        merge_other = dp_swap(merge_rows) if paired else merge_rows
        merge_own = join_halves(merge_rows, merge_other, rank, 1) if paired else merge_rows
        merge_full = col_gather(merge_own)
        cot_full = col_gather(cot_rows)
        mlp_other = dp_swap(mlp_part) if paired else mlp_part

        group_context = row_share(after(own_context, merge_other)).reshape(
            n_row * head_size, padded
        )
        context_parts = col_parts(group_context)
        mlp_other = after(mlp_other, group_context)
        expand_own, reduce_own = mlp_join(mlp_part, mlp_other, rank, n_row, units, paired)
        context_full = jnp.concatenate(
            [
                align_lanes(part, offset, near) if offset else part
                for part, offset in zip(context_parts, near)
            ],
            axis=0,
        )
        mixed1 = residual + dot(context_full, merge_full, 0, 0) + bias1
        unit2, inv2 = norm_forward(mixed1)
        normed2 = (unit2 * gain2 + shift2).astype(LOW)

        own_units = lax.dynamic_slice_in_dim(expand_bias, row * units, units, 0)
        hidden_pre = dot(normed2, expand_own, 1, 0) + own_units
        value, slope = gelu_pair(hidden_pre)
        active = value.astype(LOW)
        hidden_grad = (dot(cot_full, reduce_own, 1, 0) * slope).astype(LOW)
        normed2_total = sum_start(lambda rows: dot(rows, expand_own, 1, 1), hidden_grad)
        out_total = sum_start(
            lambda rows: dot(rows, reduce_own, 1, 1), after(active, normed2_total)
        )

        unit2_own, inv2_own, cot_own = own_rows(unit2), own_rows(inv2), own_rows(cot_full)
        normed2_parts = row_exchange(normed2_total)

        mixed_grad, mixed_low, sums = middle_rows(
            normed2_parts,
            unit2_own,
            inv2_own,
            gain2,
            cot_own,
        )
        mixed_block = row_exchange(mixed_low).reshape(block, width)
        mixed_low = col_gather(mixed_block)
        out_parts = row_exchange(after(out_total, mixed_block))
        out_rows = jnp.sum(out_parts.astype(WIDE), axis=0)
        out_rows = (own_rows(mixed1) + out_rows + bias2).astype(LOW)

        expand_grad = dot(normed2, hidden_grad, 0, 0).astype(LOW)
        reduce_grad = dot(cot_full, active, 0, 0).astype(LOW)
        expand_grad = expand_grad.reshape(n_row, feats, units)
        reduce_grad = reduce_grad.reshape(n_row, feats, units)
        mlp_grad = grad_start(jnp.concatenate([expand_grad, reduce_grad], axis=2))
        head_rows = lax.dynamic_slice_in_dim(merge_own, row * head_size, head_size, 0)
        context_grad = dot(mixed_low, head_rows, 1, 1).astype(LOW)
        mlp_moved = row_exchange(after(mlp_grad, out_parts))
        mlp_grad = grad_join(mlp_moved)
        expand_weight_grad = (
            lanes(mlp_grad[..., :units]).astype(WIDE)
        )
        reduce_weight_grad = (
            jnp.concatenate([mlp_grad[j, :, units:].T for j in range(n_row)]).astype(WIDE)
        )

        query_grad, key_grad, value_grad = attend_back(
            query_rows, key_rows, value_rows, own_context, totals, context_grad, factor, keep
        )
        joint_grad = jnp.concatenate([query_grad, key_grad, value_grad], axis=-1).astype(LOW)
        joint_bias_grad = jnp.concatenate(
            [jnp.sum(query_grad, axis=0), jnp.sum(value_grad, axis=0)]
        )
        normed1_parts = row_exchange(sum_start(lambda rows: dot(rows, joint_own, 1, 1), joint_grad))

        joint_blocks = grad_start(dot(normed1, joint_grad, 0, 0).reshape(n_row, feats, trio))
        own_mixed = lax.dynamic_slice_in_dim(mixed_low, row * feats, feats, 1)
        merge_weight_grad = dot(group_context, own_mixed, 1, 0)
        if paired:
            merge_grad_low = merge_weight_grad.astype(LOW)
            merge_weight_grad = merge_grad_low.astype(WIDE) + dp_swap(merge_grad_low).astype(WIDE)
        elif n_dp > 1:
            merge_weight_grad = lax.psum(merge_weight_grad, "dp")

        hidden_sum = jnp.pad(
            jnp.sum(hidden_grad, axis=0, dtype=WIDE), (0, -units % feats)
        ).reshape(-1, feats)
        packed, ends = final_rows(
            normed1_parts,
            own_rows(unit1),
            own_rows(inv1),
            gain1,
            mixed_grad,
            sums,
            hidden_sum,
            out_rows,
            joint_blocks,
        )
        final = row_exchange(packed)
        vectors = final[:, 2 * span : ends]
        joint_blocks = grad_join(final[:, ends:, :trio])
        joint_weight_grad = lanes(joint_blocks).astype(WIDE)
        partial = jnp.sum(merge_wide(vectors[:, :15]), axis=0)
        hidden_all = merge_wide(vectors[:, 15 : 15 + 3 * hidden_sum.shape[0]]).reshape(n_row, -1)[:, :units].reshape(-1)
        local = jnp.concatenate([hidden_all, joint_bias_grad])
        local = jnp.pad(local, (0, -local.shape[0] % feats)).reshape(-1, feats)
        local = jnp.concatenate(
            [partial, jnp.sum(cotangent.astype(WIDE), axis=0)[None], local], axis=0
        )
        spread_in = jnp.concatenate(
            [final[:, : 2 * span].reshape(2 * block, feats), split_wide(local)], axis=0
        )
        shared = lax.all_gather(spread_in, "col")
        spread = shared[:, : 2 * block].reshape(n_col, n_row, 2 * span, feats)
        outputs = spread[:, :, :span].reshape(padded, feats)[:tokens]
        inputs_grad = spread[:, :, span:].reshape(padded, feats)[:tokens].astype(WIDE)
        shared = merge_wide(shared[:, 2 * block :])
        vector_sums = jnp.concatenate([jnp.sum(shared[:, :5], axis=0), pick(shared, col)[5:]])
        if paired:
            vector_sums = vector_sums + dp_swap(vector_sums)
        elif n_dp > 1:
            vector_sums = lax.psum(vector_sums, "dp")
        reduce_bias_grad = vector_sums[5]
        own_sums = vector_sums[6:].reshape(-1)
        mid_gain_grad, mid_shift_grad, merge_bias_grad, pre_gain_grad, pre_shift_grad = [
            vector_sums[i] for i in range(5)
        ]
        tail = n_row * units
        expand_bias_grad = own_sums[:tail]
        joint_bias_grad = own_sums[tail : tail + 2 * head_size].reshape(joint_bias.shape)
        return (
            outputs,
            inputs_grad,
            pre_gain_grad,
            pre_shift_grad,
            joint_weight_grad,
            joint_bias_grad,
            merge_weight_grad,
            merge_bias_grad,
            mid_gain_grad,
            mid_shift_grad,
            expand_weight_grad,
            expand_bias_grad,
            reduce_weight_grad,
            reduce_bias_grad,
        )

    return body


def solution(mesh):
    in_specs = (
        P("dp", "row"),
        P("row"),
        P("row"),
        P("row", "col"),
        P("col", "row", None),
        P("col", "row"),
        P("row"),
        P("row"),
        P("row"),
        P("row", "col"),
        P("col"),
        P("col", "row"),
        P("row"),
        P("dp", "row"),
    )
    out_specs = (
        P("dp", "row"),
        P("dp", "row"),
        P("row"),
        P("row"),
        P("row", "col"),
        P("col", "row", None),
        P("col", "row"),
        P("row"),
        P("row"),
        P("row"),
        P("row", "col"),
        P("col"),
        P("col", "row"),
        P("row"),
    )
    body = make_body(mesh.shape["dp"], mesh.shape["row"], mesh.shape["col"])

    return jax.shard_map(body, mesh=mesh, in_specs=in_specs, out_specs=out_specs, check_vma=False)
```
